32 devices in a mesh: seq: 8 (over z, y), rep: 4 (over x, core).
Axes of the slice: x: 2, y: 2, z: 4, core: 2. Of those that a mesh axis runs over, the one named last changes fastest.
Arguments:
- reference_acts: bfloat16 [2048, 1536], P('seq'), may hold values from -6 to 6
- owners: int32 [128, 1], P('seq'), may hold values from 0 to 7; in each aligned block of 16 rows (0 to 15, 16 to 31, ...) at most 4 rows name the same one
- offsets: int32 [128], P('seq'), may hold values from 0 to 255
- codes: int32 [128], P('seq'), may hold values from 0 to 3
- base_delta: bfloat16 [4, 1536], replicated, may hold values from -6 to 6
- gain_one: bfloat16 [1536], replicated, may hold values from 0.25 to 1.75
- conv_one: bfloat16 [3, 1536, 768], replicated, may hold values from -0.09375 to 0.09375
- proj_one: bfloat16 [768, 1536], replicated, may hold values from -0.21875 to 0.21875
- gain_two: bfloat16 [1536], replicated, may hold values from 0.25 to 1.75
- conv_two: bfloat16 [3, 1536, 768], replicated, may hold values from -0.09375 to 0.09375
- proj_two: bfloat16 [768, 1536], replicated, may hold values from -0.21875 to 0.21875
- head_weight: bfloat16 [1536, 4096], P(None, 'rep'), may hold values from -0.15625 to 0.15625
- head_bias: bfloat16 [4096], P('rep'), may hold values from -1 to 1
Outputs:
- scores: float32 [128, 4096], P('seq', 'rep')
The draws below stay inside these ranges and needn't reach their ends.
Inputs may be any that keep to these rules, and one draw needn't show every extreme that they name: `owners`: no window is named by more than 4 variants of the list of one index of seq, a bound that some block reaches.
All inputs are finite; a program needn't handle non-finite values.
Results may differ from the reference program's by a relative error of at most 0.017.
Values may be sent and summed in bfloat16 or wider, within the bound.
No kernel may reach another device: no remote copies, remote signals or barrier semaphores. Data moves between devices by JAX's collectives and lax.ppermute only.
A program may use at most 128 MiB of HBM per device.

```python
import math
import jax
import jax.numpy as jnp
import numpy as np
from jax import lax

C = 1536
HALF = 768
D1 = 8
D2 = 64
WIN = 256
V_DEV = 16
CAP = 4
VARIANTS = 128
GENOME = 2048
TRACKS = 4096
N_SEQ = 8


def place_ends(array, stream_key, low, largest):
    shape = array.shape
    index_at = [jax.random.randint(jax.random.fold_in(stream_key, axis), (), 0, shape[axis]) for axis in range(len(shape))]
    array = array.at[tuple(index_at)].set(low)
    longest = shape.index(max(shape))
    index_at[longest] = (index_at[longest] + 1) % shape[longest]
    return array.at[tuple(index_at)].set(largest)


def block_levels(stream_key, shape, shards, least, high):
    factor_of = 1.0
    for axis_at, blocks in shards:
        heights = jax.random.uniform(jax.random.fold_in(jax.random.fold_in(stream_key, 6), axis_at), (blocks,), jnp.float32, least / len(shards), high / len(shards))
        factor_of = factor_of * jnp.repeat(jnp.exp(heights), shape[axis_at] // blocks).reshape((-1,) + (1,) * (len(shape) - 1 - axis_at))
    return factor_of


def shared_out(key, own, number, rows, amount, top, bound, slope):
    ranking = jax.random.permutation(key, amount)
    heavy_load, usual = load_shares(amount, rows * top, bound, slope, True), load_shares(amount, rows * top, bound, slope, False)
    places = jnp.arange(amount)

    def named(lengths, turn):
        used = int((lengths > 0).sum())
        fixed = max(1, used // 4)
        moved = fixed + (places - fixed + turn * (used - fixed)) % max(1, amount - fixed)
        return jnp.zeros((amount,), jnp.int32).at[ranking[jnp.where(places < fixed, places, moved)]].set(jnp.asarray(lengths, jnp.int32))

    lengths = jnp.where(number % 4 == 0, named(heavy_load, number // 4), named(usual, number - number // 4 - 1))
    mixed = jax.random.permutation(jax.random.fold_in(own, 3), amount)
    donor, taker = mixed[0:amount // 2 * 2:2], mixed[1:amount // 2 * 2:2]
    room = jnp.minimum(lengths[donor] - 1, bound - lengths[taker]) // 2
    room = jnp.where((donor == ranking[0]) | (taker == ranking[0]) | (lengths[taker] == 0), 0, jnp.maximum(room, 0))
    moved = jax.random.randint(jax.random.fold_in(own, 4), (amount // 2,), 0, 1 << 20) % (room + 1)
    lengths = lengths.at[donor].add(-moved).at[taker].add(moved)
    items = jnp.searchsorted(jnp.cumsum(lengths), jnp.arange(rows * top), side="right").astype(jnp.int32)
    listing = items.reshape(top, rows).T
    listing = listing[jax.random.permutation(jax.random.fold_in(own, 1), rows)]
    turn = jax.random.randint(jax.random.fold_in(own, 2), (rows, 1), 0, top)
    return jnp.take_along_axis(listing, (jnp.arange(top)[None, :] + turn) % top, axis=1)


def load_shares(amount, total, most, skew, full):
    portions = [(1 << 20) // math.isqrt(standing ** skew) + 1 for standing in range(1, amount + 1)]
    largest = most if full else min(most, max(-(-total // amount), total * portions[0] // sum(portions)))
    least = 1 if total - largest >= amount - 1 else 0
    holding, spare = [largest] + [least] * (amount - 1), total - largest - least * (amount - 1)
    while spare > 0:
        movable = [i for i in range(1, amount) if holding[i] < largest] or [i for i in range(1, amount) if holding[i] < most]
        pool, remaining = sum([portions[i] for i in movable]), spare
        for i in movable:
            extra = min(most - holding[i], max(1, remaining * portions[i] // pool), spare)
            holding[i] = holding[i] + extra
            spare = spare - extra
    return np.array(holding)


def noise(key, extent, deviation, limit, shards=(), kind=jnp.bfloat16):
    drawn = jax.random.normal(key, extent, jnp.float32) * deviation
    if len(shards) > 0:
        drawn = block_levels(key, extent, shards, -0.22, 0.18) * drawn
    return jnp.clip(drawn, min=-limit, max=limit).astype(kind)


def setup_inputs(seed: int = 0) -> dict:
    splits = jax.random.split(jax.random.key(seed), 14)
    reference_acts = noise(splits[0], (GENOME, C), 1.0, 6.0, ((0, 8),))
    owners_keys = jax.random.split(jax.random.fold_in(splits[1], 1), VARIANTS // V_DEV)
    owners_turns = jax.random.permutation(jax.random.fold_in(splits[1], 3), VARIANTS // V_DEV)
    owners = jax.vmap(lambda own, number: shared_out(jax.random.fold_in(splits[1], 2), own, number, V_DEV, N_SEQ, 1, CAP, 2))(owners_keys, owners_turns).reshape((VARIANTS, 1))
    offsets = place_ends(jax.random.randint(splits[2], (VARIANTS,), 0, WIN), jax.random.fold_in(splits[2], 1), 0, WIN - 1).astype(jnp.int32)
    codes = place_ends(jax.random.randint(splits[3], (VARIANTS,), 0, 4), jax.random.fold_in(splits[3], 1), 0, 3).astype(jnp.int32)
    base_delta = noise(splits[4], (4, C), 1.0, 6.0)
    gain_one = jnp.clip(1.0 + 0.15 * jax.random.normal(splits[5], (C,), jnp.float32), 0.25, 1.75).astype(jnp.bfloat16)
    conv_one = noise(splits[6], (3, C, HALF), (3 * C) ** -0.5, 0.09375)
    proj_one = noise(splits[7], (HALF, C), HALF ** -0.5, 0.21875)
    gain_two = jnp.clip(1.0 + 0.15 * jax.random.normal(splits[8], (C,), jnp.float32), 0.25, 1.75).astype(jnp.bfloat16)
    conv_two = noise(splits[9], (3, C, HALF), (3 * C) ** -0.5, 0.09375)
    proj_two = noise(splits[10], (HALF, C), HALF ** -0.5, 0.21875)
    head_weight = noise(splits[11], (C, TRACKS), C ** -0.5, 0.15625, ((1, 4),))
    head_bias = jnp.clip(jax.random.uniform(splits[12], (TRACKS,), jnp.float32, -1.0, 1.0) * block_levels(splits[12], (TRACKS,), ((0, 4),), -0.4, 0.0), -1.0, 1.0).astype(jnp.bfloat16)
    return {"reference_acts": reference_acts, "owners": owners, "offsets": offsets, "codes": codes, "base_delta": base_delta, "gain_one": gain_one, "conv_one": conv_one, "proj_one": proj_one, "gain_two": gain_two, "conv_two": conv_two, "proj_two": proj_two, "head_weight": head_weight, "head_bias": head_bias}


def normed(values, gain):
    scale = lax.rsqrt(lax.optimization_barrier(jnp.mean(values * values, axis=-1, keepdims=True)) + 1e-05)
    return (values * scale * gain.astype(jnp.float32)).astype(jnp.bfloat16)

def matmul(left, weight):
    flat = jnp.dot(left.reshape(-1, left.shape[-1]), weight, preferred_element_type=jnp.float32)
    return flat.reshape(left.shape[:-1] + (weight.shape[1],))

def dilated(inputs, taps, axis):
    length = inputs.shape[axis] - 2
    total = matmul(lax.slice_in_dim(inputs, 0, length, axis=axis), taps[0])
    for tap in range(1, 3):
        total = total + matmul(lax.slice_in_dim(inputs, tap, tap + length, axis=axis), taps[tap])
    return total

def cut_bins(padded, local_base, reach):
    steps_a = (jnp.arange(5, dtype=jnp.int32) - 2) * D1
    steps_m = (jnp.arange(5, dtype=jnp.int32) - 2) * D2
    index = reach + local_base[:, None, None] + steps_a[None, :, None] + steps_m[None, None, :]
    return padded[index]

def bins_inside(base, genome):
    steps_j = (jnp.arange(3, dtype=jnp.int32) - 1) * D1
    steps_i = (jnp.arange(3, dtype=jnp.int32) - 1) * D2
    where_bin = base[:, None, None] + steps_j[None, :, None] + steps_i[None, None, :]
    return ((where_bin >= 0) & (where_bin < genome)).astype(jnp.float32)

def trunk(gathered, codes, base, genome, base_delta, gain_one, conv_one, proj_one, gain_two, conv_two, proj_two):
    plain = gathered.astype(jnp.float32)
    table_hot = (codes[:, None] == jnp.arange(4, dtype=jnp.int32)[None, :]).astype(jnp.float32)
    bump = jnp.dot(table_hot, base_delta.astype(jnp.float32), precision=lax.Precision.HIGHEST)
    centre = plain[:, :, 2, :].at[:, 2, :].add(bump)
    first_ref = dilated(normed(plain, gain_one), conv_one, 1)
    first_alt = dilated(normed(centre, gain_one), conv_one, 1)
    hidden_ref = plain[:, 1:4] + matmul(jax.nn.gelu(first_ref).astype(jnp.bfloat16), proj_one)
    hidden_alt = centre[:, 1:4] + matmul(jax.nn.gelu(first_alt).astype(jnp.bfloat16), proj_one)
    steps_j = (jnp.arange(3, dtype=jnp.int32) - 1) * D1
    steps_m = (jnp.arange(5, dtype=jnp.int32) - 2) * D2
    where_bin = base[:, None, None] + steps_j[None, :, None] + steps_m[None, None, :]
    keep = (where_bin >= 0) & (where_bin < genome)
    hidden_ref = jnp.where(keep[..., None], hidden_ref, 0.0).astype(jnp.bfloat16)
    hidden_alt = jnp.where(keep[:, :, 2, None], hidden_alt, 0.0).astype(jnp.bfloat16)
    grid_alt = hidden_ref.at[:, :, 2, :].set(hidden_alt)
    both = jnp.stack([grid_alt, hidden_ref], axis=1)
    second = dilated(normed(both.astype(jnp.float32), gain_two), conv_two, 3)
    result = both[:, :, :, 1:4].astype(jnp.float32) + matmul(jax.nn.gelu(second).astype(jnp.bfloat16), proj_two)
    return result.astype(jnp.bfloat16)

def score(features, inside, head_weight, head_bias):
    logits = matmul(features, head_weight) + head_bias.astype(jnp.float32)
    cover = jax.nn.softplus(logits)
    change = (cover[:, 0] - cover[:, 1]) * inside[..., None]
    return lax.optimization_barrier(jnp.sum(change, axis=(1, 2)))

def reference(reference_acts, owners, offsets, codes, base_delta, gain_one, conv_one, proj_one, gain_two, conv_two, proj_two, head_weight, head_bias):
    genome = reference_acts.shape[0]
    reach = 2 * (D1 + D2)
    padded = jnp.pad(reference_acts, ((reach, reach), (0, 0)))
    base = (owners[:, 0] * WIN + offsets).astype(jnp.int32)
    gathered = cut_bins(padded, base, reach)
    features = trunk(gathered, codes, base, genome, base_delta, gain_one, conv_one, proj_one, gain_two, conv_two, proj_two)
    return score(features, bins_inside(base, genome), head_weight, head_bias)
```

```python
import functools

import jax
import jax.numpy as jnp
from jax import lax
from jax.experimental import pallas as pl
from jax.experimental.pallas import tpu as pltpu
from jax.sharding import PartitionSpec as P

D1 = 8
D2 = 64
REACH = 2 * (D1 + D2)
EPS = 1e-05
NT = 256
F32 = jnp.float32
BF16 = jnp.bfloat16


def gelu(x):
    inner = 0.7978845608028654 * (x + 0.044715 * (x * x * x))
    return x * (0.5 * (1.0 + jnp.tanh(inner)))


def softplus(x):
    return jnp.maximum(x, 0.0) + jnp.log1p(jnp.exp(-jnp.abs(x)))


def trunk_kernel(
    slots,
    half_cap,
    genome,
    desc_ref,
    acts_ref,
    halo_ref,
    pair_ref,
    delta_ref,
    gain1_ref,
    gain2_ref,
    bias_ref,
    pair_bias_ref,
    conv1_ref,
    proj1_ref,
    conv2_ref,
    proj2_ref,
    head_ref,
    pair_head_ref,
    out_ref,
    xp,
    w1,
    p1,
    w2,
    p2,
    hw,
    fields,
    xg,
    xalt,
    n1,
    g,
    h1,
    n2,
    h2,
    delta_v,
    gain1_v,
    gain2_v,
    bias_v,
    pair_bias_v,
    sem,
):
    S = slots
    lists = desc_ref.shape[0]
    width, C = acts_ref.shape
    half = p1.shape[0]
    tracks = head_ref.shape[1]
    here = lax.axis_index("seq")
    core = lax.rem(lax.axis_index("rep"), 2)
    other = 1 - core

    def rows(start):
        return pl.ds(pl.multiple_of(start, 16), REACH)

    copies = [
        (acts_ref, xp.at[pl.ds(REACH, width)]),
        (halo_ref, xp.at[rows(core * (REACH + width))]),
        (pair_ref, xp.at[rows(other * (REACH + width))]),
        (conv1_ref.at[0], w1.at[0]),
        (conv1_ref.at[1], w1.at[1]),
        (conv1_ref.at[2], w1.at[2]),
        (proj1_ref, p1),
        (conv2_ref.at[0], w2.at[0]),
        (conv2_ref.at[1], w2.at[1]),
        (conv2_ref.at[2], w2.at[2]),
        (proj2_ref, p2),
        (head_ref, hw.at[core]),
        (pair_head_ref, hw.at[other]),
        (delta_ref, delta_v),
        (gain1_ref, gain1_v),
        (gain2_ref, gain2_v),
        (bias_ref, bias_v),
        (pair_bias_ref, pair_bias_v),
    ]
    copies = [pltpu.make_async_copy(a, b, sem.at[i]) for i, (a, b) in enumerate(copies)]
    for copy in copies[13:] + copies[:13]:
        copy.start()

    for s in range(lists):
        for f in range(3):
            fields[f, s * half_cap : (s + 1) * half_cap, :] = jnp.broadcast_to(
                desc_ref[s, f : f + 1, :], (half_cap, 128)
            )
    hit = fields[0] == here
    upper = (
        lax.broadcasted_iota(jnp.int32, (128, 128), 0)
        < lax.broadcasted_iota(jnp.int32, (128, 128), 1)
    )
    rank = jnp.dot(
        jnp.where(hit, 1.0, 0.0).astype(BF16),
        jnp.where(upper, 1.0, 0.0).astype(BF16),
        preferred_element_type=F32,
    )
    want = core * half_cap + lax.rem(lax.broadcasted_iota(jnp.int32, (S, 128), 0), half_cap)
    chosen = hit & (rank == want.astype(F32))
    offset = jnp.sum(jnp.where(chosen, fields[1].astype(F32), 0.0), axis=1, keepdims=True)
    offset = offset.astype(jnp.int32)
    code = jnp.sum(jnp.where(chosen, fields[2].astype(F32), 0.0), axis=1, keepdims=True)
    where_bin = here * width + offset

    def inside(j, m):
        at = where_bin + (j * D1 + m * D2)
        return (at >= 0) & (at < genome)

    span = 2 * width
    low = 2 * (D1 + D2) * 2 + width - span
    column = lax.broadcasted_iota(jnp.int32, (S, span), 1)

    def pick(a, m, base):
        return jnp.where(column == offset + (a * D1 + m * D2 - base), 1.0, 0.0).astype(BF16)

    early = jnp.concatenate([pick(a, m, 0) for a in range(5) for m in range(4)], axis=0)
    late = jnp.concatenate([pick(a, 4, low) for a in range(5)], axis=0)
    for copy in copies[13:] + copies[:3]:
        copy.wait()
    for n in range(C // NT):
        at = pl.ds(n * NT, NT)
        first = jnp.dot(early, xp[:span, at], preferred_element_type=F32).astype(BF16)
        last = jnp.dot(late, xp[low : low + span, at], preferred_element_type=F32).astype(BF16)
        for a in range(5):
            xg[a * 5 * S : (a * 5 + 4) * S, at] = first[a * 4 * S : (a + 1) * 4 * S]
            xg[(a * 5 + 4) * S : (a * 5 + 5) * S, at] = last[a * S : (a + 1) * S]
    bump = jnp.zeros((S, C), F32)
    for k in range(4):
        bump = jnp.where(code == k, delta_v[k : k + 1, :].astype(F32), bump)
    xalt[...] = xg[12 * S : 13 * S, :].astype(F32) + bump

    def normed(values, gain):
        scale = lax.rsqrt(jnp.mean(values * values, axis=-1, keepdims=True) + EPS)
        return (values * scale * gain).astype(BF16)

    gain1 = gain1_v[...].astype(F32).reshape(1, C)
    for b in range(25):
        n1[b * S : (b + 1) * S, :] = normed(xg[b * S : (b + 1) * S, :].astype(F32), gain1)
    n1[25 * S : 26 * S, :] = normed(xalt[...], gain1)

    for copy in copies[3:6]:
        copy.wait()
    for n in range(half // NT):
        at = pl.ds(n * NT, NT)
        taps = []
        for k in range(3):
            left = jnp.concatenate(
                [n1[k * 5 * S : (k + 3) * 5 * S, :], n1[25 * S : 26 * S, :]], axis=0
            )
            taps.append(jnp.dot(left, w1[k, :, at], preferred_element_type=F32))
        total = (taps[0] + taps[1]) + taps[2]
        g[: 15 * S, at] = gelu(total[: 15 * S]).astype(BF16)
        for j in range(3):
            base = (j * 5 + 2) * S
            parts = [
                taps[k][15 * S : 16 * S] if k == 2 - j else taps[k][base : base + S]
                for k in range(3)
            ]
            g[(15 + j) * S : (16 + j) * S, at] = gelu((parts[0] + parts[1]) + parts[2]).astype(BF16)

    copies[6].wait()
    for n in range(C // NT):
        at = pl.ds(n * NT, NT)
        delta = jnp.dot(g[...], p1[:, at], preferred_element_type=F32)
        for j in range(3):
            for m in range(5):
                b = j * 5 + m
                x = xg[(b + 5) * S : (b + 6) * S, at].astype(F32)
                h = jnp.where(inside(j - 1, m - 2), x + delta[b * S : (b + 1) * S], 0.0)
                h1[(m * 3 + j) * S : (m * 3 + j + 1) * S, at] = h.astype(BF16)
            b = 15 + j
            x = xalt[:, at] if j == 1 else xg[(j * 5 + 7) * S : (j * 5 + 8) * S, at].astype(F32)
            h = jnp.where(inside(j - 1, 0), x + delta[b * S : (b + 1) * S], 0.0)
            h1[b * S : (b + 1) * S, at] = h.astype(BF16)
    gain2 = gain2_v[...].astype(F32).reshape(1, C)
    for b in range(18):
        n2[b * S : (b + 1) * S, :] = normed(h1[b * S : (b + 1) * S, :].astype(F32), gain2)

    for copy in copies[7:10]:
        copy.wait()
    for n in range(half // NT):
        at = pl.ds(n * NT, NT)
        taps = []
        for k in range(3):
            left = jnp.concatenate(
                [n2[k * 3 * S : (k + 3) * 3 * S, :], n2[15 * S : 18 * S, :]], axis=0
            )
            taps.append(jnp.dot(left, w2[k, :, at], preferred_element_type=F32))
        total = (taps[0] + taps[1]) + taps[2]
        g[: 9 * S, at] = gelu(total[: 9 * S]).astype(BF16)
        for i in range(3):
            base = i * 3 * S
            parts = [
                taps[k][9 * S : 12 * S] if k == 2 - i else taps[k][base : base + 3 * S]
                for k in range(3)
            ]
            g[(9 + 3 * i) * S : (12 + 3 * i) * S, at] = gelu(
                (parts[0] + parts[1]) + parts[2]
            ).astype(BF16)

    copies[10].wait()
    for n in range(C // NT):
        at = pl.ds(n * NT, NT)
        delta = jnp.dot(g[...], p2[:, at], preferred_element_type=F32)
        for i in range(3):
            plain = h1[(i + 1) * 3 * S : (i + 2) * 3 * S, at].astype(F32)
            changed = h1[15 * S : 18 * S, at].astype(F32) if i == 1 else plain
            lo = i * 3 * S
            h2[lo : lo + 3 * S, at] = (plain + delta[lo : lo + 3 * S]).astype(BF16)
            lo += 9 * S
            h2[lo : lo + 3 * S, at] = (changed + delta[lo : lo + 3 * S]).astype(BF16)

    for copy in copies[11:13]:
        copy.wait()
    keep = [
        jnp.where(inside(j - 1, i - 1), 1.0, 0.0) for i in range(3) for j in range(3)
    ]
    for side in range(2):
        bias = jnp.where(core == side, bias_v[...].astype(F32), pair_bias_v[...].astype(F32)).reshape(1, tracks)
        for n in range(tracks // NT):
            at = pl.ds(n * NT, NT)
            logits = jnp.dot(h2[...], hw[side, :, at], preferred_element_type=F32)
            cover = softplus(logits + bias[:, n * NT : (n + 1) * NT])
            score = jnp.zeros((S, NT), F32)
            for b in range(9):
                change = cover[(9 + b) * S : (10 + b) * S] - cover[b * S : (b + 1) * S]
                score = score + change * keep[b]
            per = tracks // 128
            for t in range(NT // 128):
                start = side * S * per + n * (NT // 128) + t
                out_ref[pl.ds(start, S, stride=per), :] = score[:, t * 128 : (t + 1) * 128]


def trunk_and_head(desc, acts, halo, pair, delta, gain1, gain2, bias, pair_bias, weights, genome, half_cap):
    conv1, proj1, conv2, proj2, head, pair_head = weights
    lists = desc.shape[0]
    S = lists * half_cap
    width, C = acts.shape
    half = proj1.shape[0]
    tracks = head.shape[1]
    vm = pl.BlockSpec(memory_space=pltpu.VMEM)
    hbm = pl.BlockSpec(memory_space=pltpu.HBM)
    free = pl.BlockSpec(memory_space=pl.ANY)
    macs = S * (48 * C * half + 18 * C * half + 36 * C * half + 18 * C * half + 36 * C * tracks)
    acts, delta, gain1, gain2, bias, conv1, proj1, conv2, proj2, head = (
        pltpu.with_memory_space_constraint(a, pltpu.HBM)
        for a in (acts, delta, gain1, gain2, bias, conv1, proj1, conv2, proj2, head)
    )
    return pl.pallas_call(
        functools.partial(trunk_kernel, S, half_cap, genome),
        out_shape=jax.ShapeDtypeStruct((2 * S * tracks // 128, 128), F32),
        in_specs=[vm, hbm, free, free] + [hbm] * 4 + [free] + [hbm] * 5 + [free],
        out_specs=vm,
        scratch_shapes=[
            pltpu.VMEM((width + 2 * REACH, C), BF16),
            pltpu.VMEM((3, C, half), BF16),
            pltpu.VMEM((half, C), BF16),
            pltpu.VMEM((3, C, half), BF16),
            pltpu.VMEM((half, C), BF16),
            pltpu.VMEM((2, C, tracks), BF16),
            pltpu.VMEM((3, S, 128), jnp.int32),
            pltpu.VMEM((25 * S, C), BF16),
            pltpu.VMEM((S, C), F32),
            pltpu.VMEM((26 * S, C), BF16),
            pltpu.VMEM((18 * S, half), BF16),
            pltpu.VMEM((18 * S, C), BF16),
            pltpu.VMEM((18 * S, C), BF16),
            pltpu.VMEM((18 * S, C), BF16),
            pltpu.VMEM(delta.shape, BF16),
            pltpu.VMEM(gain1.shape, BF16),
            pltpu.VMEM(gain2.shape, BF16),
            pltpu.VMEM(bias.shape, BF16),
            pltpu.VMEM(bias.shape, BF16),
            pltpu.SemaphoreType.DMA((18,)),
        ],
        compiler_params=pltpu.CompilerParams(vmem_limit_bytes=36 * 1024 * 1024),
        cost_estimate=pl.CostEstimate(
            flops=2 * macs, bytes_accessed=28 * 1024 * 1024, transcendentals=S * 18 * (half * 2 + tracks * 4)
        ),
        name="trunk_and_head",
    )(desc, acts, halo, pair, delta, gain1, gain2, bias, pair_bias, conv1, proj1, conv2, proj2, head, pair_head)


def return_kernel(n_seq, half_cap, owners_ref, got_ref, out_ref, tiles):
    count, tracks = out_ref.shape
    per = tracks // 128
    for v in range(count):
        mine = owners_ref[v]
        rank = jnp.int32(0)
        for u in range(v):
            rank = rank + jnp.where(owners_ref[u] == mine, 1, 0)
        side = lax.div(rank, half_cap)
        row = ((side * n_seq + mine) * half_cap + (rank - side * half_cap)) * per
        tiles[v * per : (v + 1) * per, :] = got_ref[pl.ds(pl.multiple_of(row, 8), per), :]
    for t in range(per):
        out_ref[:, t * 128 : (t + 1) * 128] = tiles[pl.ds(t, count, stride=per), :]


def per_device(
    reference_acts,
    owners,
    offsets,
    codes,
    base_delta,
    gain_one,
    conv_one,
    proj_one,
    gain_two,
    conv_two,
    proj_two,
    head_weight,
    head_bias,
):
    n_seq = lax.axis_size("seq")
    n_rep = lax.axis_size("rep")
    width = reference_acts.shape[0]
    genome = width * n_seq
    core = lax.axis_index("rep") % 2
    vcount = owners.shape[0]
    half_cap = max(2, 2 * vcount // n_seq) // 2
    tracks = head_weight.shape[1]
    swap = [(r, r ^ 1) for r in range(n_rep)]
    steps = [(i, r, i + 1 - 2 * (r % 2)) for i in range(n_seq) for r in range(n_rep)]
    edges = [(i * n_rep + r, j * n_rep + r) for i, r, j in steps if 0 <= j < n_seq]

    owner = owners[:, 0]
    fields = jnp.stack([owner, offsets, codes])
    fields = jnp.pad(fields, ((0, 5), (0, 128 - vcount)), constant_values=-1)
    edge = lax.dynamic_slice_in_dim(reference_acts, (1 - core) * (width - REACH), REACH, 0)
    halo = lax.ppermute(edge, ("seq", "rep"), edges)
    pair_head = lax.ppermute(head_weight, "rep", swap)
    pair_bias = lax.ppermute(head_bias, "rep", swap)
    desc = lax.all_to_all(
        jnp.broadcast_to(fields[None], (n_seq, 8, 128)), "seq", split_axis=0, concat_axis=0, tiled=True
    )
    halo, desc = lax.optimization_barrier((halo, desc))
    pair = lax.ppermute(halo, "rep", swap)
    scores = trunk_and_head(
        desc,
        reference_acts,
        halo,
        pair,
        base_delta,
        gain_one,
        gain_two,
        head_bias,
        pair_bias,
        (conv_one, proj_one, conv_two, proj_two, head_weight, pair_head),
        genome,
        half_cap,
    )
    per = tracks // 128
    groups = [
        [s * n_rep + x + c for c in range(2) for s in range(n_seq)] for x in range(0, n_rep, 2)
    ]
    got = lax.all_to_all(
        scores.reshape(2 * n_seq, half_cap * per, 128),
        ("seq", "rep"),
        split_axis=0,
        concat_axis=0,
        axis_index_groups=groups,
        tiled=True,
    ).reshape(2 * n_seq * half_cap * per, 128)
    return pl.pallas_call(
        functools.partial(return_kernel, n_seq, half_cap),
        out_shape=jax.ShapeDtypeStruct((vcount, tracks), F32),
        in_specs=[pl.BlockSpec(memory_space=pltpu.SMEM), pl.BlockSpec(memory_space=pltpu.VMEM)],
        out_specs=pl.BlockSpec(memory_space=pltpu.VMEM),
        scratch_shapes=[pltpu.VMEM((vcount * per, 128), F32)],
        name="pick_scores",
    )(owner, got)


def solution(mesh):
    return jax.shard_map(
        per_device,
        mesh=mesh,
        in_specs=(
            P("seq", None),
            P("seq", None),
            P("seq"),
            P("seq"),
            P(),
            P(),
            P(),
            P(),
            P(),
            P(),
            P(),
            P(None, "rep"),
            P("rep"),
        ),
        out_specs=P("seq", "rep"),
        check_vma=False,
    )
```

```python
import functools

import jax
import jax.numpy as jnp
from jax import lax
from jax.experimental import pallas as pl
from jax.experimental.pallas import tpu as pltpu
from jax.sharding import PartitionSpec as P

D1 = 8
D2 = 64
REACH = 2 * (D1 + D2)
EPS = 1e-05
NT = 256
F32 = jnp.float32
BF16 = jnp.bfloat16


def gelu(x):
    inner = 0.7978845608028654 * (x + 0.044715 * (x * x * x))
    return x * (0.5 * (1.0 + jnp.tanh(inner)))


def softplus(x):
    return jnp.maximum(x, 0.0) + jnp.log1p(jnp.exp(-jnp.abs(x)))


def slot_kernel(half_cap, desc_ref, slots_ref, fields):
    lists = desc_ref.shape[0]
    S = lists * half_cap
    here = lax.axis_index("seq")
    core = lax.rem(lax.axis_index("rep"), 2)
    for s in range(lists):
        for f in range(3):
            fields[f, s * half_cap : (s + 1) * half_cap, :] = jnp.broadcast_to(
                desc_ref[s, f : f + 1, :], (half_cap, 128)
            )
    hit = fields[0] == here
    upper = (
        lax.broadcasted_iota(jnp.int32, (128, 128), 0)
        < lax.broadcasted_iota(jnp.int32, (128, 128), 1)
    )
    rank = jnp.dot(
        jnp.where(hit, 1.0, 0.0).astype(BF16),
        jnp.where(upper, 1.0, 0.0).astype(BF16),
        preferred_element_type=F32,
    )
    want = core * half_cap + lax.rem(lax.broadcasted_iota(jnp.int32, (S, 128), 0), half_cap)
    chosen = hit & (rank == want.astype(F32))
    offset = jnp.sum(jnp.where(chosen, fields[1].astype(F32), 0.0), axis=1, keepdims=True)
    offset = offset.astype(jnp.int32)
    code = jnp.sum(jnp.where(chosen, fields[2].astype(F32), 0.0), axis=1, keepdims=True)
    lane = lax.broadcasted_iota(jnp.int32, (S, 128), 1)
    slots_ref[...] = jnp.where(lane == 0, offset, code.astype(jnp.int32))


def slot_table(desc, half_cap):
    S = desc.shape[0] * half_cap
    vm = pl.BlockSpec(memory_space=pltpu.VMEM)
    return pl.pallas_call(
        functools.partial(slot_kernel, half_cap),
        out_shape=jax.ShapeDtypeStruct((S, 128), jnp.int32),
        in_specs=[vm],
        out_specs=vm,
        scratch_shapes=[pltpu.VMEM((3, S, 128), jnp.int32)],
        compiler_params=pltpu.CompilerParams(vmem_limit_bytes=1024 * 1024),
        cost_estimate=pl.CostEstimate(flops=1_000_000, bytes_accessed=40_000, transcendentals=0),
        name="slot_table",
    )(desc)


def trunk_kernel(
    slots,
    genome,
    slots_ref,
    acts_ref,
    halo_ref,
    pair_ref,
    delta_ref,
    gain1_ref,
    gain2_ref,
    bias_ref,
    pair_bias_ref,
    conv1_ref,
    proj1_ref,
    conv2_ref,
    proj2_ref,
    head_ref,
    pair_head_ref,
    out_ref,
    xg,
    xalt,
    n1,
    g,
    h1,
    n2,
    h2,
):
    S = slots
    width, C = acts_ref.shape
    half = proj1_ref.shape[0]
    tracks = head_ref.shape[1]
    here = lax.axis_index("seq")
    core = lax.rem(lax.axis_index("rep"), 2)
    other = 1 - core

    offset = slots_ref[:, 0:1]
    code = slots_ref[:, 1:2]
    where_bin = here * width + offset

    def inside(j, m):
        at = where_bin + (j * D1 + m * D2)
        return (at >= 0) & (at < genome)

    sources = (
        (halo_ref, core * (REACH + width)),
        (acts_ref, REACH),
        (pair_ref, other * (REACH + width)),
    )
    picks = []
    for source, base in sources:
        column = lax.broadcasted_iota(jnp.int32, (S, source.shape[0]), 1) + base - offset
        picks.append(
            jnp.concatenate(
                [
                    jnp.where(column == a * D1 + m * D2, 1.0, 0.0).astype(BF16)
                    for a in range(5)
                    for m in range(5)
                ],
                axis=0,
            )
        )
    for n in range(C // NT):
        at = pl.ds(n * NT, NT)
        parts = [
            jnp.dot(picked, source[:, at], preferred_element_type=F32)
            for picked, (source, _) in zip(picks, sources)
        ]
        xg[:, at] = ((parts[0] + parts[1]) + parts[2]).astype(BF16)
    bump = jnp.zeros((S, C), F32)
    for k in range(4):
        bump = jnp.where(code == k, delta_ref[k : k + 1, :].astype(F32), bump)
    xalt[...] = xg[12 * S : 13 * S, :].astype(F32) + bump

    def normed(values, gain):
        scale = lax.rsqrt(jnp.mean(values * values, axis=-1, keepdims=True) + EPS)
        return (values * scale * gain).astype(BF16)

    gain1 = gain1_ref[...].astype(F32).reshape(1, C)
    for b in range(25):
        n1[b * S : (b + 1) * S, :] = normed(xg[b * S : (b + 1) * S, :].astype(F32), gain1)
    n1[25 * S : 26 * S, :] = normed(xalt[...], gain1)

    for n in range(half // NT):
        at = pl.ds(n * NT, NT)
        taps = []
        for k in range(3):
            left = jnp.concatenate(
                [n1[k * 5 * S : (k + 3) * 5 * S, :], n1[25 * S : 26 * S, :]], axis=0
            )
            taps.append(jnp.dot(left, conv1_ref[k, :, at], preferred_element_type=F32))
        total = (taps[0] + taps[1]) + taps[2]
        g[: 15 * S, at] = gelu(total[: 15 * S]).astype(BF16)
        for j in range(3):
            base = (j * 5 + 2) * S
            parts = [
                taps[k][15 * S : 16 * S] if k == 2 - j else taps[k][base : base + S]
                for k in range(3)
            ]
            g[(15 + j) * S : (16 + j) * S, at] = gelu((parts[0] + parts[1]) + parts[2]).astype(BF16)

    for n in range(C // NT):
        at = pl.ds(n * NT, NT)
        delta = jnp.dot(g[...], proj1_ref[:, at], preferred_element_type=F32)
        for j in range(3):
            for m in range(5):
                b = j * 5 + m
                x = xg[(b + 5) * S : (b + 6) * S, at].astype(F32)
                h = jnp.where(inside(j - 1, m - 2), x + delta[b * S : (b + 1) * S], 0.0)
                h1[(m * 3 + j) * S : (m * 3 + j + 1) * S, at] = h.astype(BF16)
            b = 15 + j
            x = xalt[:, at] if j == 1 else xg[(j * 5 + 7) * S : (j * 5 + 8) * S, at].astype(F32)
            h = jnp.where(inside(j - 1, 0), x + delta[b * S : (b + 1) * S], 0.0)
            h1[b * S : (b + 1) * S, at] = h.astype(BF16)
    gain2 = gain2_ref[...].astype(F32).reshape(1, C)
    for b in range(18):
        n2[b * S : (b + 1) * S, :] = normed(h1[b * S : (b + 1) * S, :].astype(F32), gain2)

    for n in range(half // NT):
        at = pl.ds(n * NT, NT)
        taps = []
        for k in range(3):
            left = jnp.concatenate(
                [n2[k * 3 * S : (k + 3) * 3 * S, :], n2[15 * S : 18 * S, :]], axis=0
            )
            taps.append(jnp.dot(left, conv2_ref[k, :, at], preferred_element_type=F32))
        total = (taps[0] + taps[1]) + taps[2]
        g[: 9 * S, at] = gelu(total[: 9 * S]).astype(BF16)
        for i in range(3):
            base = i * 3 * S
            parts = [
                taps[k][9 * S : 12 * S] if k == 2 - i else taps[k][base : base + 3 * S]
                for k in range(3)
            ]
            g[(9 + 3 * i) * S : (12 + 3 * i) * S, at] = gelu(
                (parts[0] + parts[1]) + parts[2]
            ).astype(BF16)

    for n in range(C // NT):
        at = pl.ds(n * NT, NT)
        delta = jnp.dot(g[...], proj2_ref[:, at], preferred_element_type=F32)
        for i in range(3):
            plain = h1[(i + 1) * 3 * S : (i + 2) * 3 * S, at].astype(F32)
            changed = h1[15 * S : 18 * S, at].astype(F32) if i == 1 else plain
            lo = i * 3 * S
            h2[lo : lo + 3 * S, at] = (plain + delta[lo : lo + 3 * S]).astype(BF16)
            lo += 9 * S
            h2[lo : lo + 3 * S, at] = (changed + delta[lo : lo + 3 * S]).astype(BF16)

    keep = [
        jnp.where(inside(j - 1, i - 1), 1.0, 0.0) for i in range(3) for j in range(3)
    ]
    for side in range(2):
        bias = (bias_ref, pair_bias_ref)[side][...].astype(F32).reshape(1, tracks)
        weight = (head_ref, pair_head_ref)[side]
        block = (core if side == 0 else other) * (S * (tracks // 128))
        for n in range(tracks // NT):
            at = pl.ds(n * NT, NT)
            logits = jnp.dot(h2[...], weight[:, at], preferred_element_type=F32)
            cover = softplus(logits + bias[:, n * NT : (n + 1) * NT])
            score = jnp.zeros((S, NT), F32)
            for b in range(9):
                change = cover[(9 + b) * S : (10 + b) * S] - cover[b * S : (b + 1) * S]
                score = score + change * keep[b]
            per = tracks // 128
            for t in range(NT // 128):
                start = block + n * (NT // 128) + t
                out_ref[pl.ds(start, S, stride=per), :] = score[:, t * 128 : (t + 1) * 128]


def trunk_and_head(table, acts, halo, pair, delta, gain1, gain2, bias, pair_bias, weights, genome):
    conv1, proj1, conv2, proj2, head, pair_head = weights
    S = table.shape[0]
    width, C = acts.shape
    half = proj1.shape[0]
    tracks = head.shape[1]
    vm = pl.BlockSpec(memory_space=pltpu.VMEM)
    macs = S * (48 * C * half + 18 * C * half + 36 * C * half + 18 * C * half + 36 * C * tracks)
    operands = [
        pltpu.with_memory_space_constraint(a, pltpu.VMEM)
        for a in (table, acts, halo, pair, delta, gain1, gain2, bias, pair_bias) + weights
    ]
    return pl.pallas_call(
        functools.partial(trunk_kernel, S, genome),
        out_shape=jax.ShapeDtypeStruct((2 * S * tracks // 128, 128), F32),
        in_specs=[vm] * len(operands),
        out_specs=vm,
        scratch_shapes=[
            pltpu.VMEM((25 * S, C), BF16),
            pltpu.VMEM((S, C), F32),
            pltpu.VMEM((26 * S, C), BF16),
            pltpu.VMEM((18 * S, half), BF16),
            pltpu.VMEM((18 * S, C), BF16),
            pltpu.VMEM((18 * S, C), BF16),
            pltpu.VMEM((18 * S, C), BF16),
        ],
        compiler_params=pltpu.CompilerParams(vmem_limit_bytes=12 * 1024 * 1024),
        cost_estimate=pl.CostEstimate(
            flops=2 * macs, bytes_accessed=28 * 1024 * 1024, transcendentals=S * 18 * (half * 2 + tracks * 4)
        ),
        name="trunk_and_head",
    )(*operands)


def return_kernel(n_seq, half_cap, owners_ref, got_ref, out_ref, tiles):
    count, tracks = out_ref.shape
    per = tracks // 128
    for v in range(count):
        mine = owners_ref[v]
        rank = jnp.int32(0)
        for u in range(v):
            rank = rank + jnp.where(owners_ref[u] == mine, 1, 0)
        side = lax.div(rank, half_cap)
        row = ((side * n_seq + mine) * half_cap + (rank - side * half_cap)) * per
        tiles[v * per : (v + 1) * per, :] = got_ref[pl.ds(pl.multiple_of(row, 8), per), :]
    for t in range(per):
        out_ref[:, t * 128 : (t + 1) * 128] = tiles[pl.ds(t, count, stride=per), :]


def first_kernel(acts_ref, owners_ref, offsets_ref, codes_ref, edge_ref, out_ref, rows, sem):
    core = lax.rem(lax.axis_index("rep"), 2)
    lists = out_ref.shape[0]
    count = owners_ref.shape[1]
    reach = edge_ref.shape[0]
    begin = pl.multiple_of((1 - core) * (acts_ref.shape[0] - reach), 16)
    copies = [pltpu.make_async_copy(acts_ref.at[pl.ds(begin, reach)], edge_ref, sem.at[3])]
    copies += [
        pltpu.make_async_copy(ref, row, sem.at[i])
        for i, (ref, row) in enumerate(zip((owners_ref, offsets_ref, codes_ref), rows))
    ]
    for copy in copies:
        copy.start()
    out_ref[...] = jnp.full(out_ref.shape, -1, jnp.int32)
    for copy in copies:
        copy.wait()
    for f in range(3):
        row = rows[f][...].reshape(1, count)
        for s in range(lists):
            out_ref[s, f : f + 1, 0:count] = row


def edge_and_lists(acts, owner, offsets, codes, lists):
    hbm = pl.BlockSpec(memory_space=pltpu.HBM)
    vm = pl.BlockSpec(memory_space=pltpu.VMEM)
    args = [pltpu.with_memory_space_constraint(a, pltpu.HBM) for a in (acts, owner, offsets, codes)]
    return pl.pallas_call(
        first_kernel,
        out_shape=(
            jax.ShapeDtypeStruct((REACH, acts.shape[1]), BF16),
            jax.ShapeDtypeStruct((lists, 8, 128), jnp.int32),
        ),
        in_specs=[hbm, hbm, hbm, hbm],
        out_specs=(vm, vm),
        scratch_shapes=[
            [pltpu.VMEM(a.shape, jnp.int32) for a in args[1:]],
            pltpu.SemaphoreType.DMA((4,)),
        ],
        compiler_params=pltpu.CompilerParams(vmem_limit_bytes=2 * 1024 * 1024),
        cost_estimate=pl.CostEstimate(flops=20_000_000_000, bytes_accessed=900_000, transcendentals=0),
        name="edge_and_lists",
    )(*args)


def per_device(
    reference_acts,
    owners,
    offsets,
    codes,
    base_delta,
    gain_one,
    conv_one,
    proj_one,
    gain_two,
    conv_two,
    proj_two,
    head_weight,
    head_bias,
):
    n_seq = lax.axis_size("seq")
    n_rep = lax.axis_size("rep")
    width = reference_acts.shape[0]
    genome = width * n_seq
    vcount = owners.shape[0]
    half_cap = max(2, 2 * vcount // n_seq) // 2
    tracks = head_weight.shape[1]
    swap = [(r, r ^ 1) for r in range(n_rep)]
    steps = [(i, r, i + 1 - 2 * (r % 2)) for i in range(n_seq) for r in range(n_rep)]
    edges = [(i * n_rep + r, j * n_rep + r) for i, r, j in steps if 0 <= j < n_seq]

    owner = owners[:, 0]
    edge, fields = edge_and_lists(
        reference_acts, owners.reshape(1, vcount), offsets, codes, n_seq
    )
    halo = lax.ppermute(edge, ("seq", "rep"), edges)
    pair_head = lax.ppermute(head_weight, "rep", swap)
    pair_bias = lax.ppermute(head_bias, "rep", swap)
    desc = lax.all_to_all(fields, "seq", split_axis=0, concat_axis=0, tiled=True)
    halo, desc = lax.optimization_barrier((halo, desc))
    pair = lax.ppermute(halo, "rep", swap)
    scores = trunk_and_head(
        slot_table(desc, half_cap),
        reference_acts,
        halo,
        pair,
        base_delta,
        gain_one,
        gain_two,
        head_bias,
        pair_bias,
        (conv_one, proj_one, conv_two, proj_two, head_weight, pair_head),
        genome,
    )
    per = tracks // 128
    groups = [
        [s * n_rep + x + c for c in range(2) for s in range(n_seq)] for x in range(0, n_rep, 2)
    ]
    got = lax.all_to_all(
        scores.reshape(2 * n_seq, half_cap * per, 128),
        ("seq", "rep"),
        split_axis=0,
        concat_axis=0,
        axis_index_groups=groups,
        tiled=True,
    ).reshape(2 * n_seq * half_cap * per, 128)
    got = pltpu.with_memory_space_constraint(got, pltpu.VMEM)
    return pl.pallas_call(
        functools.partial(return_kernel, n_seq, half_cap),
        out_shape=jax.ShapeDtypeStruct((vcount, tracks), F32),
        in_specs=[pl.BlockSpec(memory_space=pltpu.SMEM), pl.BlockSpec(memory_space=pltpu.VMEM)],
        out_specs=pl.BlockSpec(memory_space=pltpu.VMEM),
        scratch_shapes=[pltpu.VMEM((vcount * per, 128), F32)],
        compiler_params=pltpu.CompilerParams(vmem_limit_bytes=2 * 1024 * 1024),
        name="pick_scores",
    )(owner, got)


def solution(mesh):
    return jax.shard_map(
        per_device,
        mesh=mesh,
        in_specs=(
            P("seq", None),
            P("seq", None),
            P("seq"),
            P("seq"),
            P(),
            P(),
            P(),
            P(),
            P(),
            P(),
            P(),
            P(None, "rep"),
            P("rep"),
        ),
        out_specs=P("seq", "rep"),
        check_vma=False,
    )
```

```python
import functools

import jax
import jax.numpy as jnp
from jax import lax
from jax.experimental import pallas as pl
from jax.experimental.pallas import tpu as pltpu
from jax.sharding import PartitionSpec as P

D1 = 8
D2 = 64
REACH = 2 * (D1 + D2)
EPS = 1e-05
NT = 256
F32 = jnp.float32
BF16 = jnp.bfloat16


def gelu(x):
    inner = 0.7978845608028654 * (x + 0.044715 * (x * x * x))
    return x * (0.5 * (1.0 + jnp.tanh(inner)))


def softplus(x):
    return jnp.maximum(x, 0.0) + jnp.log(1.0 + jnp.exp(-jnp.abs(x)))


def pick_rows(offset, count, base):
    S = offset.shape[0]
    column = lax.broadcasted_iota(jnp.int32, (S, count), 1) + base - offset
    return jnp.concatenate(
        [
            jnp.where(column == a * D1 + m * D2, 1.0, 0.0).astype(BF16)
            for a in range(5)
            for m in range(5)
        ],
        axis=0,
    )


def slot_kernel(
    half_cap, per, desc_ref, acts_ref, halo_ref, slots_ref, places_ref, early_ref, fields
):
    lists = desc_ref.shape[0]
    S = lists * half_cap
    here = lax.axis_index("seq")
    core = lax.rem(lax.axis_index("rep"), 2)
    for s in range(lists):
        for f in range(3):
            fields[f, s * half_cap : (s + 1) * half_cap, :] = jnp.broadcast_to(
                desc_ref[s, f : f + 1, :], (half_cap, 128)
            )
    hit = fields[0] == here
    upper = (
        lax.broadcasted_iota(jnp.int32, (128, 128), 0)
        < lax.broadcasted_iota(jnp.int32, (128, 128), 1)
    )
    rank = jnp.dot(
        jnp.where(hit, 1.0, 0.0).astype(BF16),
        jnp.where(upper, 1.0, 0.0).astype(BF16),
        preferred_element_type=F32,
    )
    want = core * half_cap + lax.rem(lax.broadcasted_iota(jnp.int32, (S, 128), 0), half_cap)
    chosen = hit & (rank == want.astype(F32))
    offset = jnp.sum(jnp.where(chosen, fields[1].astype(F32), 0.0), axis=1, keepdims=True)
    offset = offset.astype(jnp.int32)
    code = jnp.sum(jnp.where(chosen, fields[2].astype(F32), 0.0), axis=1, keepdims=True)
    lane = lax.broadcasted_iota(jnp.int32, (S, 128), 1)
    slots_ref[...] = jnp.where(lane == 0, offset, code.astype(jnp.int32))

    width, C = acts_ref.shape
    own = pick_rows(offset, width, REACH)
    near = pick_rows(offset, halo_ref.shape[0], core * (REACH + width))
    for n in range(C // NT):
        at = pl.ds(n * NT, NT)
        found = jnp.dot(own, acts_ref[:, at], preferred_element_type=F32)
        found = found + jnp.dot(near, halo_ref[:, at], preferred_element_type=F32)
        early_ref[:, at] = found.astype(BF16)

    window = lax.broadcasted_iota(jnp.int32, (lists, 128), 0)
    hit = jnp.broadcast_to(desc_ref[here, 0:1, :], (lists, 128)) == window
    rank = jnp.dot(
        jnp.where(hit, 1.0, 0.0).astype(BF16),
        jnp.where(upper, 1.0, 0.0).astype(BF16),
        preferred_element_type=F32,
    ).astype(jnp.int32)
    side = jnp.where(rank >= half_cap, 1, 0)
    place = ((side * lists + window) * half_cap + (rank - side * half_cap)) * per
    place = jnp.sum(jnp.where(hit, place.astype(F32), 0.0), axis=0, keepdims=True)
    places_ref[...] = jnp.broadcast_to(place.astype(jnp.int32), places_ref.shape)


def slot_table(desc, acts, halo, half_cap, per):
    S = desc.shape[0] * half_cap
    acts, halo = (pltpu.with_memory_space_constraint(a, pltpu.VMEM) for a in (acts, halo))
    vm = pl.BlockSpec(memory_space=pltpu.VMEM)
    return pl.pallas_call(
        functools.partial(slot_kernel, half_cap, per),
        out_shape=(
            jax.ShapeDtypeStruct((S, 128), jnp.int32),
            jax.ShapeDtypeStruct((8, 128), jnp.int32),
            jax.ShapeDtypeStruct((25 * S, acts.shape[1]), BF16),
        ),
        in_specs=[vm, vm, vm],
        out_specs=(vm, vm, vm),
        scratch_shapes=[pltpu.VMEM((3, S, 128), jnp.int32)],
        compiler_params=pltpu.CompilerParams(vmem_limit_bytes=4 * 1024 * 1024),
        cost_estimate=pl.CostEstimate(
            flops=50 * S * acts.shape[1] * (acts.shape[0] + REACH), bytes_accessed=2_000_000, transcendentals=0
        ),
        name="slot_table",
    )(desc, acts, halo)


def trunk_kernel(
    slots,
    width,
    genome,
    slots_ref,
    early_ref,
    pair_ref,
    delta_ref,
    gain1_ref,
    gain2_ref,
    bias_ref,
    pair_bias_ref,
    conv1_ref,
    proj1_ref,
    conv2_ref,
    proj2_ref,
    head_ref,
    pair_head_ref,
    out_ref,
    xg,
    xalt,
    n1,
    g,
    h1,
    n2,
    h2,
):
    S = slots
    C = early_ref.shape[1]
    half = proj1_ref.shape[0]
    tracks = head_ref.shape[1]
    here = lax.axis_index("seq")
    core = lax.rem(lax.axis_index("rep"), 2)
    other = 1 - core

    offset = slots_ref[:, 0:1]
    code = slots_ref[:, 1:2]
    where_bin = here * width + offset

    def inside(j, m):
        at = where_bin + (j * D1 + m * D2)
        return (at >= 0) & (at < genome)

    chosen = pick_rows(offset, pair_ref.shape[0], other * (REACH + width))
    for n in range(C // NT):
        at = pl.ds(n * NT, NT)
        found = jnp.dot(chosen, pair_ref[:, at], preferred_element_type=F32)
        xg[:, at] = (found + early_ref[:, at].astype(F32)).astype(BF16)
    bump = jnp.zeros((S, C), F32)
    for k in range(4):
        bump = jnp.where(code == k, delta_ref[k : k + 1, :].astype(F32), bump)
    xalt[...] = xg[12 * S : 13 * S, :].astype(F32) + bump

    def normed(values, gain):
        scale = lax.rsqrt(jnp.mean(values * values, axis=-1, keepdims=True) + EPS)
        return (values * scale * gain).astype(BF16)

    gain1 = gain1_ref[...].astype(F32).reshape(1, C)
    for b in range(25):
        n1[b * S : (b + 1) * S, :] = normed(xg[b * S : (b + 1) * S, :].astype(F32), gain1)
    n1[25 * S : 26 * S, :] = normed(xalt[...], gain1)

    for n in range(half // NT):
        at = pl.ds(n * NT, NT)
        taps = []
        for k in range(3):
            left = jnp.concatenate(
                [n1[k * 5 * S : (k + 3) * 5 * S, :], n1[25 * S : 26 * S, :]], axis=0
            )
            taps.append(jnp.dot(left, conv1_ref[k, :, at], preferred_element_type=F32))
        total = (taps[0] + taps[1]) + taps[2]
        g[: 15 * S, at] = gelu(total[: 15 * S]).astype(BF16)
        for j in range(3):
            base = (j * 5 + 2) * S
            parts = [
                taps[k][15 * S : 16 * S] if k == 2 - j else taps[k][base : base + S]
                for k in range(3)
            ]
            g[(15 + j) * S : (16 + j) * S, at] = gelu((parts[0] + parts[1]) + parts[2]).astype(BF16)

    for n in range(C // NT):
        at = pl.ds(n * NT, NT)
        delta = jnp.dot(g[...], proj1_ref[:, at], preferred_element_type=F32)
        for j in range(3):
            for m in range(5):
                b = j * 5 + m
                x = xg[(b + 5) * S : (b + 6) * S, at].astype(F32)
                h = jnp.where(inside(j - 1, m - 2), x + delta[b * S : (b + 1) * S], 0.0)
                h1[(m * 3 + j) * S : (m * 3 + j + 1) * S, at] = h.astype(BF16)
            b = 15 + j
            x = xalt[:, at] if j == 1 else xg[(j * 5 + 7) * S : (j * 5 + 8) * S, at].astype(F32)
            h = jnp.where(inside(j - 1, 0), x + delta[b * S : (b + 1) * S], 0.0)
            h1[b * S : (b + 1) * S, at] = h.astype(BF16)
    gain2 = gain2_ref[...].astype(F32).reshape(1, C)
    for b in range(18):
        n2[b * S : (b + 1) * S, :] = normed(h1[b * S : (b + 1) * S, :].astype(F32), gain2)

    for n in range(half // NT):
        at = pl.ds(n * NT, NT)
        taps = []
        for k in range(3):
            left = jnp.concatenate(
                [n2[k * 3 * S : (k + 3) * 3 * S, :], n2[15 * S : 18 * S, :]], axis=0
            )
            taps.append(jnp.dot(left, conv2_ref[k, :, at], preferred_element_type=F32))
        total = (taps[0] + taps[1]) + taps[2]
        g[: 9 * S, at] = gelu(total[: 9 * S]).astype(BF16)
        for i in range(3):
            base = i * 3 * S
            parts = [
                taps[k][9 * S : 12 * S] if k == 2 - i else taps[k][base : base + 3 * S]
                for k in range(3)
            ]
            g[(9 + 3 * i) * S : (12 + 3 * i) * S, at] = gelu(
                (parts[0] + parts[1]) + parts[2]
            ).astype(BF16)

    for n in range(C // NT):
        at = pl.ds(n * NT, NT)
        delta = jnp.dot(g[...], proj2_ref[:, at], preferred_element_type=F32)
        for i in range(3):
            plain = h1[(i + 1) * 3 * S : (i + 2) * 3 * S, at].astype(F32)
            changed = h1[15 * S : 18 * S, at].astype(F32) if i == 1 else plain
            lo = i * 3 * S
            h2[lo : lo + 3 * S, at] = (plain + delta[lo : lo + 3 * S]).astype(BF16)
            lo += 9 * S
            h2[lo : lo + 3 * S, at] = (changed + delta[lo : lo + 3 * S]).astype(BF16)

    keep = [
        jnp.where(inside(j - 1, i - 1), 1.0, 0.0) for i in range(3) for j in range(3)
    ]
    for side in range(2):
        bias = (bias_ref, pair_bias_ref)[side][...].astype(F32).reshape(1, tracks)
        weight = (head_ref, pair_head_ref)[side]
        block = (core if side == 0 else other) * (S * (tracks // 128))
        for n in range(tracks // NT):
            at = pl.ds(n * NT, NT)
            logits = jnp.dot(h2[...], weight[:, at], preferred_element_type=F32)
            cover = softplus(logits + bias[:, n * NT : (n + 1) * NT])
            score = jnp.zeros((S, NT), F32)
            for b in range(9):
                change = cover[(9 + b) * S : (10 + b) * S] - cover[b * S : (b + 1) * S]
                score = score + change * keep[b]
            per = tracks // 128
            for t in range(NT // 128):
                start = block + n * (NT // 128) + t
                out_ref[pl.ds(start, S, stride=per), :] = score[:, t * 128 : (t + 1) * 128]


def trunk_and_head(table, early, pair, delta, gain1, gain2, bias, pair_bias, weights, width, genome):
    conv1, proj1, conv2, proj2, head, pair_head = weights
    S = table.shape[0]
    C = early.shape[1]
    half = proj1.shape[0]
    tracks = head.shape[1]
    vm = pl.BlockSpec(memory_space=pltpu.VMEM)
    macs = S * (48 * C * half + 18 * C * half + 36 * C * half + 18 * C * half + 36 * C * tracks)
    operands = [
        pltpu.with_memory_space_constraint(a, pltpu.VMEM)
        for a in (table, early, pair, delta, gain1, gain2, bias, pair_bias) + weights
    ]
    return pl.pallas_call(
        functools.partial(trunk_kernel, S, width, genome),
        out_shape=jax.ShapeDtypeStruct((2 * S * tracks // 128, 128), F32),
        in_specs=[vm] * len(operands),
        out_specs=vm,
        scratch_shapes=[
            pltpu.VMEM((25 * S, C), BF16),
            pltpu.VMEM((S, C), F32),
            pltpu.VMEM((26 * S, C), BF16),
            pltpu.VMEM((18 * S, half), BF16),
            pltpu.VMEM((18 * S, C), BF16),
            pltpu.VMEM((18 * S, C), BF16),
            pltpu.VMEM((18 * S, C), BF16),
        ],
        compiler_params=pltpu.CompilerParams(vmem_limit_bytes=12 * 1024 * 1024),
        cost_estimate=pl.CostEstimate(
            flops=2 * macs, bytes_accessed=28 * 1024 * 1024, transcendentals=S * 18 * (half * 2 + tracks * 4)
        ),
        name="trunk_and_head",
    )(*operands)


def return_kernel(places_ref, got_ref, out_ref, tiles):
    count, tracks = out_ref.shape
    per = tracks // 128
    for v in range(count):
        row = pl.multiple_of(places_ref[v], 8)
        tiles[v * per : (v + 1) * per, :] = got_ref[pl.ds(row, per), :]
    for t in range(per):
        out_ref[:, t * 128 : (t + 1) * 128] = tiles[pl.ds(t, count, stride=per), :]


def pack_kernel(owners_ref, offsets_ref, codes_ref, out_ref, rows, sem):
    lists = out_ref.shape[0]
    count = owners_ref.shape[1]
    copies = [
        pltpu.make_async_copy(ref, row, sem.at[i])
        for i, (ref, row) in enumerate(zip((owners_ref, offsets_ref, codes_ref), rows))
    ]
    for copy in copies:
        copy.start()
    out_ref[...] = jnp.full(out_ref.shape, -1, jnp.int32)
    for copy in copies:
        copy.wait()
    for f in range(3):
        row = rows[f][...].reshape(1, count)
        for s in range(lists):
            out_ref[s, f : f + 1, 0:count] = row


def pack_lists(owner, offsets, codes, lists):
    hbm = pl.BlockSpec(memory_space=pltpu.HBM)
    args = [pltpu.with_memory_space_constraint(a, pltpu.HBM) for a in (owner, offsets, codes)]
    return pl.pallas_call(
        pack_kernel,
        out_shape=jax.ShapeDtypeStruct((lists, 8, 128), jnp.int32),
        in_specs=[hbm, hbm, hbm],
        out_specs=pl.BlockSpec(memory_space=pltpu.VMEM),
        scratch_shapes=[
            [pltpu.VMEM(a.shape, jnp.int32) for a in args],
            pltpu.SemaphoreType.DMA((3,)),
        ],
        compiler_params=pltpu.CompilerParams(vmem_limit_bytes=1024 * 1024),
        cost_estimate=pl.CostEstimate(flops=20_000_000_000, bytes_accessed=40_000, transcendentals=0),
        name="pack_lists",
    )(*args)


def per_device(
    reference_acts,
    owners,
    offsets,
    codes,
    base_delta,
    gain_one,
    conv_one,
    proj_one,
    gain_two,
    conv_two,
    proj_two,
    head_weight,
    head_bias,
):
    n_seq = lax.axis_size("seq")
    n_rep = lax.axis_size("rep")
    width = reference_acts.shape[0]
    genome = width * n_seq
    vcount = owners.shape[0]
    half_cap = max(2, 2 * vcount // n_seq) // 2
    tracks = head_weight.shape[1]
    swap = [(r, r ^ 1) for r in range(n_rep)]
    steps = [(i, r, i + 1 - 2 * (r % 2)) for i in range(n_seq) for r in range(n_rep)]
    edges = [(i * n_rep + r, j * n_rep + r) for i, r, j in steps if 0 <= j < n_seq]

    fields = pack_lists(owners.reshape(1, vcount), offsets, codes, n_seq)
    core = lax.axis_index("rep") % 2
    edge = lax.dynamic_slice_in_dim(reference_acts, (1 - core) * (width - REACH), REACH, 0)
    halo = lax.ppermute(edge, ("seq", "rep"), edges)
    pair_head = lax.ppermute(head_weight, "rep", swap)
    pair_bias = lax.ppermute(head_bias, "rep", swap)
    desc = lax.all_to_all(fields, "seq", split_axis=0, concat_axis=0, tiled=True)
    halo, desc = lax.optimization_barrier((halo, desc))
    pair = lax.ppermute(halo, "rep", swap)
    per = tracks // 128
    slots, places, early = slot_table(desc, reference_acts, halo, half_cap, per)
    scores = trunk_and_head(
        slots,
        early,
        pair,
        base_delta,
        gain_one,
        gain_two,
        head_bias,
        pair_bias,
        (conv_one, proj_one, conv_two, proj_two, head_weight, pair_head),
        width,
        genome,
    )
    groups = [
        [s * n_rep + x + c for c in range(2) for s in range(n_seq)] for x in range(0, n_rep, 2)
    ]
    got = lax.all_to_all(
        scores.reshape(2 * n_seq, half_cap * per, 128),
        ("seq", "rep"),
        split_axis=0,
        concat_axis=0,
        axis_index_groups=groups,
        tiled=True,
    ).reshape(2 * n_seq * half_cap * per, 128)
    got = pltpu.with_memory_space_constraint(got, pltpu.VMEM)
    return pl.pallas_call(
        return_kernel,
        out_shape=jax.ShapeDtypeStruct((vcount, tracks), F32),
        in_specs=[pl.BlockSpec(memory_space=pltpu.SMEM), pl.BlockSpec(memory_space=pltpu.VMEM)],
        out_specs=pl.BlockSpec(memory_space=pltpu.VMEM),
        scratch_shapes=[pltpu.VMEM((vcount * per, 128), F32)],
        compiler_params=pltpu.CompilerParams(vmem_limit_bytes=2 * 1024 * 1024),
        name="pick_scores",
    )(places[0], got)


def solution(mesh):
    return jax.shard_map(
        per_device,
        mesh=mesh,
        in_specs=(
            P("seq", None),
            P("seq", None),
            P("seq"),
            P("seq"),
            P(),
            P(),
            P(),
            P(),
            P(),
            P(),
            P(),
            P(None, "rep"),
            P("rep"),
        ),
        out_specs=P("seq", "rep"),
        check_vma=False,
    )
```

```python
import functools

import jax
import jax.numpy as jnp
from jax import lax
from jax.experimental import pallas as pl
from jax.experimental.pallas import tpu as pltpu
from jax.sharding import PartitionSpec as P

D1 = 8
D2 = 64
REACH = 2 * (D1 + D2)
EPS = 1e-05
NT = 256
F32 = jnp.float32
BF16 = jnp.bfloat16


def gelu(x):
    inner = 0.7978845608028654 * (x + 0.044715 * (x * x * x))
    return x * (0.5 * (1.0 + jnp.tanh(inner)))


def softplus(x):
    return jnp.maximum(x, 0.0) + jnp.log(1.0 + jnp.exp(-jnp.abs(x)))


def pick_rows(offset, count, base):
    S = offset.shape[0]
    column = lax.broadcasted_iota(jnp.int32, (S, count), 1) + base - offset
    return jnp.concatenate(
        [
            jnp.where(column == a * D1 + m * D2, 1.0, 0.0).astype(BF16)
            for a in range(5)
            for m in range(5)
        ],
        axis=0,
    )


def slot_kernel(
    half_cap, per, desc_ref, acts_ref, halo_ref, slots_ref, places_ref, early_ref, fields
):
    lists = desc_ref.shape[0]
    S = lists * half_cap
    here = lax.axis_index("seq")
    core = lax.rem(lax.axis_index("rep"), 2)
    for s in range(lists):
        for f in range(3):
            fields[f, s * half_cap : (s + 1) * half_cap, :] = jnp.broadcast_to(
                desc_ref[s, f : f + 1, :], (half_cap, 128)
            )
    hit = fields[0] == here
    upper = (
        lax.broadcasted_iota(jnp.int32, (128, 128), 0)
        < lax.broadcasted_iota(jnp.int32, (128, 128), 1)
    )
    rank = jnp.dot(
        jnp.where(hit, 1.0, 0.0).astype(BF16),
        jnp.where(upper, 1.0, 0.0).astype(BF16),
        preferred_element_type=F32,
    )
    want = core * half_cap + lax.rem(lax.broadcasted_iota(jnp.int32, (S, 128), 0), half_cap)
    chosen = hit & (rank == want.astype(F32))
    offset = jnp.sum(jnp.where(chosen, fields[1].astype(F32), 0.0), axis=1, keepdims=True)
    offset = offset.astype(jnp.int32)
    code = jnp.sum(jnp.where(chosen, fields[2].astype(F32), 0.0), axis=1, keepdims=True)
    lane = lax.broadcasted_iota(jnp.int32, (S, 128), 1)
    slots_ref[...] = jnp.where(lane == 0, offset, code.astype(jnp.int32))

    width, C = acts_ref.shape
    own = pick_rows(offset, width, REACH)
    near = pick_rows(offset, halo_ref.shape[0], core * (REACH + width))
    for n in range(C // NT):
        at = pl.ds(n * NT, NT)
        found = jnp.dot(own, acts_ref[:, at], preferred_element_type=F32)
        found = found + jnp.dot(near, halo_ref[:, at], preferred_element_type=F32)
        early_ref[:, at] = found.astype(BF16)

    window = lax.broadcasted_iota(jnp.int32, (lists, 128), 0)
    hit = jnp.broadcast_to(desc_ref[here, 0:1, :], (lists, 128)) == window
    rank = jnp.dot(
        jnp.where(hit, 1.0, 0.0).astype(BF16),
        jnp.where(upper, 1.0, 0.0).astype(BF16),
        preferred_element_type=F32,
    ).astype(jnp.int32)
    side = jnp.where(rank >= half_cap, 1, 0)
    place = ((side * lists + window) * half_cap + (rank - side * half_cap)) * per
    place = jnp.sum(jnp.where(hit, place.astype(F32), 0.0), axis=0, keepdims=True)
    places_ref[...] = jnp.broadcast_to(place.astype(jnp.int32), places_ref.shape)


def slot_table(desc, acts, halo, half_cap, per):
    S = desc.shape[0] * half_cap
    acts, halo = (pltpu.with_memory_space_constraint(a, pltpu.VMEM) for a in (acts, halo))
    vm = pl.BlockSpec(memory_space=pltpu.VMEM)
    return pl.pallas_call(
        functools.partial(slot_kernel, half_cap, per),
        out_shape=(
            jax.ShapeDtypeStruct((S, 128), jnp.int32),
            jax.ShapeDtypeStruct((8, 128), jnp.int32),
            jax.ShapeDtypeStruct((25 * S, acts.shape[1]), BF16),
        ),
        in_specs=[vm, vm, vm],
        out_specs=(vm, vm, vm),
        scratch_shapes=[pltpu.VMEM((3, S, 128), jnp.int32)],
        compiler_params=pltpu.CompilerParams(vmem_limit_bytes=4 * 1024 * 1024),
        cost_estimate=pl.CostEstimate(
            flops=50 * S * acts.shape[1] * (acts.shape[0] + REACH), bytes_accessed=2_000_000, transcendentals=0
        ),
        name="slot_table",
    )(desc, acts, halo)


def trunk_kernel(
    slots,
    width,
    genome,
    slots_ref,
    early_ref,
    pair_ref,
    delta_ref,
    gain1_ref,
    gain2_ref,
    bias_ref,
    pair_bias_ref,
    conv1_ref,
    proj1_ref,
    conv2_ref,
    proj2_ref,
    head_ref,
    pair_head_ref,
    out_ref,
    xg,
    xalt,
    n1,
    g,
    h1,
    n2,
    h2,
    packed,
):
    S = slots
    C = early_ref.shape[1]
    half = proj1_ref.shape[0]
    tracks = head_ref.shape[1]
    here = lax.axis_index("seq")
    core = lax.rem(lax.axis_index("rep"), 2)
    other = 1 - core

    offset = slots_ref[:, 0:1]
    code = slots_ref[:, 1:2]
    where_bin = here * width + offset

    def inside(j, m):
        at = where_bin + (j * D1 + m * D2)
        return (at >= 0) & (at < genome)

    chosen = pick_rows(offset, pair_ref.shape[0], other * (REACH + width))
    for n in range(C // NT):
        at = pl.ds(n * NT, NT)
        found = jnp.dot(chosen, pair_ref[:, at], preferred_element_type=F32)
        xg[:, at] = (found + early_ref[:, at].astype(F32)).astype(BF16)
    bump = jnp.zeros((S, C), F32)
    for k in range(4):
        bump = jnp.where(code == k, delta_ref[k : k + 1, :].astype(F32), bump)
    xalt[...] = xg[12 * S : 13 * S, :].astype(F32) + bump

    def normed(values, gain):
        scale = lax.rsqrt(jnp.mean(values * values, axis=-1, keepdims=True) + EPS)
        return (values * scale * gain).astype(BF16)

    gain1 = gain1_ref[...].astype(F32).reshape(1, C)
    for b in range(25):
        n1[b * S : (b + 1) * S, :] = normed(xg[b * S : (b + 1) * S, :].astype(F32), gain1)
    n1[25 * S : 26 * S, :] = normed(xalt[...], gain1)

    for n in range(half // NT):
        at = pl.ds(n * NT, NT)
        taps = []
        for k in range(3):
            left = jnp.concatenate(
                [n1[k * 5 * S : (k + 3) * 5 * S, :], n1[25 * S : 26 * S, :]], axis=0
            )
            taps.append(jnp.dot(left, conv1_ref[k, :, at], preferred_element_type=F32))
        total = (taps[0] + taps[1]) + taps[2]
        g[: 15 * S, at] = gelu(total[: 15 * S]).astype(BF16)
        for j in range(3):
            base = (j * 5 + 2) * S
            parts = [
                taps[k][15 * S : 16 * S] if k == 2 - j else taps[k][base : base + S]
                for k in range(3)
            ]
            g[(15 + j) * S : (16 + j) * S, at] = gelu((parts[0] + parts[1]) + parts[2]).astype(BF16)

    for n in range(C // NT):
        at = pl.ds(n * NT, NT)
        delta = jnp.dot(g[...], proj1_ref[:, at], preferred_element_type=F32)
        for j in range(3):
            for m in range(5):
                b = j * 5 + m
                x = xg[(b + 5) * S : (b + 6) * S, at].astype(F32)
                h = jnp.where(inside(j - 1, m - 2), x + delta[b * S : (b + 1) * S], 0.0)
                h1[(m * 3 + j) * S : (m * 3 + j + 1) * S, at] = h.astype(BF16)
            b = 15 + j
            x = xalt[:, at] if j == 1 else xg[(j * 5 + 7) * S : (j * 5 + 8) * S, at].astype(F32)
            h = jnp.where(inside(j - 1, 0), x + delta[b * S : (b + 1) * S], 0.0)
            h1[b * S : (b + 1) * S, at] = h.astype(BF16)
    gain2 = gain2_ref[...].astype(F32).reshape(1, C)
    for b in range(18):
        n2[b * S : (b + 1) * S, :] = normed(h1[b * S : (b + 1) * S, :].astype(F32), gain2)

    for n in range(half // NT):
        at = pl.ds(n * NT, NT)
        taps = []
        for k in range(3):
            left = jnp.concatenate(
                [n2[k * 3 * S : (k + 3) * 3 * S, :], n2[15 * S : 18 * S, :]], axis=0
            )
            taps.append(jnp.dot(left, conv2_ref[k, :, at], preferred_element_type=F32))
        total = (taps[0] + taps[1]) + taps[2]
        g[: 9 * S, at] = gelu(total[: 9 * S]).astype(BF16)
        for i in range(3):
            base = i * 3 * S
            parts = [
                taps[k][9 * S : 12 * S] if k == 2 - i else taps[k][base : base + 3 * S]
                for k in range(3)
            ]
            g[(9 + 3 * i) * S : (12 + 3 * i) * S, at] = gelu(
                (parts[0] + parts[1]) + parts[2]
            ).astype(BF16)

    for n in range(C // NT):
        at = pl.ds(n * NT, NT)
        delta = jnp.dot(g[...], proj2_ref[:, at], preferred_element_type=F32)
        for i in range(3):
            plain = h1[(i + 1) * 3 * S : (i + 2) * 3 * S, at].astype(F32)
            changed = h1[15 * S : 18 * S, at].astype(F32) if i == 1 else plain
            lo = i * 3 * S
            h2[lo : lo + 3 * S, at] = (plain + delta[lo : lo + 3 * S]).astype(BF16)
            lo += 9 * S
            h2[lo : lo + 3 * S, at] = (changed + delta[lo : lo + 3 * S]).astype(BF16)

    keep = [
        jnp.where(inside(j - 1, i - 1), 1.0, 0.0) for i in range(3) for j in range(3)
    ]
    for side in range(2):
        bias = (bias_ref, pair_bias_ref)[side][...].astype(F32).reshape(1, tracks)
        weight = (head_ref, pair_head_ref)[side]
        block = (core if side == 0 else other) * (S * (tracks // 128))
        for n in range(tracks // NT):
            at = pl.ds(n * NT, NT)
            logits = jnp.dot(h2[...], weight[:, at], preferred_element_type=F32)
            cover = softplus(logits + bias[:, n * NT : (n + 1) * NT])
            score = jnp.zeros((S, NT), F32)
            for b in range(9):
                change = cover[(9 + b) * S : (10 + b) * S] - cover[b * S : (b + 1) * S]
                score = score + change * keep[b]
            per = tracks // 128
            for t in range(NT // 128):
                start = block + n * (NT // 128) + t
                packed[pl.ds(start, S, stride=per), :] = score[:, t * 128 : (t + 1) * 128]
    out_ref[...] = packed[...].astype(BF16)


def trunk_and_head(table, early, pair, delta, gain1, gain2, bias, pair_bias, weights, width, genome):
    conv1, proj1, conv2, proj2, head, pair_head = weights
    S = table.shape[0]
    C = early.shape[1]
    half = proj1.shape[0]
    tracks = head.shape[1]
    vm = pl.BlockSpec(memory_space=pltpu.VMEM)
    macs = S * (48 * C * half + 18 * C * half + 36 * C * half + 18 * C * half + 36 * C * tracks)
    operands = [
        pltpu.with_memory_space_constraint(a, pltpu.VMEM)
        for a in (table, early, pair, delta, gain1, gain2, bias, pair_bias) + weights
    ]
    return pl.pallas_call(
        functools.partial(trunk_kernel, S, width, genome),
        out_shape=jax.ShapeDtypeStruct((2 * S * tracks // 128, 128), BF16),
        in_specs=[vm] * len(operands),
        out_specs=vm,
        scratch_shapes=[
            pltpu.VMEM((25 * S, C), BF16),
            pltpu.VMEM((S, C), F32),
            pltpu.VMEM((26 * S, C), BF16),
            pltpu.VMEM((18 * S, half), BF16),
            pltpu.VMEM((18 * S, C), BF16),
            pltpu.VMEM((18 * S, C), BF16),
            pltpu.VMEM((18 * S, C), BF16),
            pltpu.VMEM((2 * S * tracks // 128, 128), F32),
        ],
        compiler_params=pltpu.CompilerParams(vmem_limit_bytes=12 * 1024 * 1024),
        cost_estimate=pl.CostEstimate(
            flops=2 * macs, bytes_accessed=28 * 1024 * 1024, transcendentals=S * 18 * (half * 2 + tracks * 4)
        ),
        name="trunk_and_head",
    )(*operands)


def return_kernel(places_ref, got_ref, out_ref, wide, tiles):
    wide[...] = got_ref[...].astype(F32)
    count, tracks = out_ref.shape
    per = tracks // 128
    for v in range(count):
        row = pl.multiple_of(places_ref[v], 8)
        tiles[v * per : (v + 1) * per, :] = wide[pl.ds(row, per), :]
    for t in range(per):
        out_ref[:, t * 128 : (t + 1) * 128] = tiles[pl.ds(t, count, stride=per), :]


def pack_kernel(owners_ref, offsets_ref, codes_ref, out_ref, rows, sem):
    lists = out_ref.shape[0]
    count = owners_ref.shape[1]
    copies = [
        pltpu.make_async_copy(ref, row, sem.at[i])
        for i, (ref, row) in enumerate(zip((owners_ref, offsets_ref, codes_ref), rows))
    ]
    for copy in copies:
        copy.start()
    out_ref[...] = jnp.full(out_ref.shape, -1, jnp.int32)
    for copy in copies:
        copy.wait()
    for f in range(3):
        row = rows[f][...].reshape(1, count)
        for s in range(lists):
            out_ref[s, f : f + 1, 0:count] = row


def pack_lists(owner, offsets, codes, lists):
    hbm = pl.BlockSpec(memory_space=pltpu.HBM)
    args = [pltpu.with_memory_space_constraint(a, pltpu.HBM) for a in (owner, offsets, codes)]
    return pl.pallas_call(
        pack_kernel,
        out_shape=jax.ShapeDtypeStruct((lists, 8, 128), jnp.int32),
        in_specs=[hbm, hbm, hbm],
        out_specs=pl.BlockSpec(memory_space=pltpu.VMEM),
        scratch_shapes=[
            [pltpu.VMEM(a.shape, jnp.int32) for a in args],
            pltpu.SemaphoreType.DMA((3,)),
        ],
        compiler_params=pltpu.CompilerParams(vmem_limit_bytes=1024 * 1024),
        cost_estimate=pl.CostEstimate(flops=20_000_000_000, bytes_accessed=40_000, transcendentals=0),
        name="pack_lists",
    )(*args)


def per_device(
    reference_acts,
    owners,
    offsets,
    codes,
    base_delta,
    gain_one,
    conv_one,
    proj_one,
    gain_two,
    conv_two,
    proj_two,
    head_weight,
    head_bias,
):
    n_seq = lax.axis_size("seq")
    n_rep = lax.axis_size("rep")
    width = reference_acts.shape[0]
    genome = width * n_seq
    vcount = owners.shape[0]
    half_cap = max(2, 2 * vcount // n_seq) // 2
    tracks = head_weight.shape[1]
    swap = [(r, r ^ 1) for r in range(n_rep)]
    steps = [(i, r, i + 1 - 2 * (r % 2)) for i in range(n_seq) for r in range(n_rep)]
    edges = [(i * n_rep + r, j * n_rep + r) for i, r, j in steps if 0 <= j < n_seq]

    fields = pack_lists(owners.reshape(1, vcount), offsets, codes, n_seq)
    core = lax.axis_index("rep") % 2
    edge = lax.dynamic_slice_in_dim(reference_acts, (1 - core) * (width - REACH), REACH, 0)
    halo = lax.ppermute(edge, ("seq", "rep"), edges)
    pair_head = lax.ppermute(head_weight, "rep", swap)
    pair_bias = lax.ppermute(head_bias, "rep", swap)
    desc = lax.all_to_all(fields, "seq", split_axis=0, concat_axis=0, tiled=True)
    halo, desc = lax.optimization_barrier((halo, desc))
    pair = lax.ppermute(halo, "rep", swap)
    per = tracks // 128
    slots, places, early = slot_table(desc, reference_acts, halo, half_cap, per)
    scores = trunk_and_head(
        slots,
        early,
        pair,
        base_delta,
        gain_one,
        gain_two,
        head_bias,
        pair_bias,
        (conv_one, proj_one, conv_two, proj_two, head_weight, pair_head),
        width,
        genome,
    )
    groups = [
        [s * n_rep + x + c for c in range(2) for s in range(n_seq)] for x in range(0, n_rep, 2)
    ]
    got = lax.all_to_all(
        scores.reshape(2 * n_seq, half_cap * per, 128),
        ("seq", "rep"),
        split_axis=0,
        concat_axis=0,
        axis_index_groups=groups,
        tiled=True,
    ).reshape(2 * n_seq * half_cap * per, 128)
    got = pltpu.with_memory_space_constraint(got, pltpu.VMEM)
    return pl.pallas_call(
        return_kernel,
        out_shape=jax.ShapeDtypeStruct((vcount, tracks), F32),
        in_specs=[pl.BlockSpec(memory_space=pltpu.SMEM), pl.BlockSpec(memory_space=pltpu.VMEM)],
        out_specs=pl.BlockSpec(memory_space=pltpu.VMEM),
        scratch_shapes=[pltpu.VMEM(got.shape, F32), pltpu.VMEM((vcount * per, 128), F32)],
        compiler_params=pltpu.CompilerParams(vmem_limit_bytes=2 * 1024 * 1024),
        name="pick_scores",
    )(places[0], got)


def solution(mesh):
    return jax.shard_map(
        per_device,
        mesh=mesh,
        in_specs=(
            P("seq", None),
            P("seq", None),
            P("seq"),
            P("seq"),
            P(),
            P(),
            P(),
            P(),
            P(),
            P(),
            P(),
            P(None, "rep"),
            P("rep"),
        ),
        out_specs=P("seq", "rep"),
        check_vma=False,
    )
```

```python
import functools

import jax
import jax.numpy as jnp
from jax import lax
from jax.experimental import pallas as pl
from jax.experimental.pallas import tpu as pltpu
from jax.sharding import PartitionSpec as P

D1 = 8
D2 = 64
REACH = 2 * (D1 + D2)
EPS = 1e-05
NT = 256
F32 = jnp.float32
BF16 = jnp.bfloat16


def gelu(x):
    inner = 0.7978845608028654 * (x + 0.044715 * (x * x * x))
    return x * (0.5 * (1.0 + jnp.tanh(inner)))


def softplus(x):
    return jnp.maximum(x, 0.0) + jnp.log(1.0 + jnp.exp(-jnp.abs(x)))


def pick_rows(offset, count, base):
    S = offset.shape[0]
    column = lax.broadcasted_iota(jnp.int32, (S, count), 1) + base - offset
    return jnp.concatenate(
        [
            jnp.where(column == a * D1 + m * D2, 1.0, 0.0).astype(BF16)
            for a in range(5)
            for m in range(5)
        ],
        axis=0,
    )


def slot_kernel(
    half_cap, per, desc_ref, acts_ref, halo_ref, slots_ref, places_ref, early_ref, fields
):
    lists = desc_ref.shape[0]
    S = lists * half_cap
    here = lax.axis_index("seq")
    core = lax.rem(lax.axis_index("rep"), 2)
    for s in range(lists):
        for f in range(3):
            fields[f, s * half_cap : (s + 1) * half_cap, :] = jnp.broadcast_to(
                desc_ref[s, f : f + 1, :], (half_cap, 128)
            )
    hit = fields[0] == here
    upper = (
        lax.broadcasted_iota(jnp.int32, (128, 128), 0)
        < lax.broadcasted_iota(jnp.int32, (128, 128), 1)
    )
    rank = jnp.dot(
        jnp.where(hit, 1.0, 0.0).astype(BF16),
        jnp.where(upper, 1.0, 0.0).astype(BF16),
        preferred_element_type=F32,
    )
    want = core * half_cap + lax.rem(lax.broadcasted_iota(jnp.int32, (S, 128), 0), half_cap)
    chosen = hit & (rank == want.astype(F32))
    offset = jnp.sum(jnp.where(chosen, fields[1].astype(F32), 0.0), axis=1, keepdims=True)
    offset = offset.astype(jnp.int32)
    code = jnp.sum(jnp.where(chosen, fields[2].astype(F32), 0.0), axis=1, keepdims=True)
    lane = lax.broadcasted_iota(jnp.int32, (S, 128), 1)
    slots_ref[...] = jnp.where(lane == 0, offset, code.astype(jnp.int32))

    width, C = acts_ref.shape
    own = pick_rows(offset, width, REACH)
    near = pick_rows(offset, halo_ref.shape[0], core * (REACH + width))
    for n in range(C // NT):
        at = pl.ds(n * NT, NT)
        found = jnp.dot(own, acts_ref[:, at], preferred_element_type=F32)
        found = found + jnp.dot(near, halo_ref[:, at], preferred_element_type=F32)
        early_ref[:, at] = found.astype(BF16)

    window = lax.broadcasted_iota(jnp.int32, (lists, 128), 0)
    hit = jnp.broadcast_to(desc_ref[here, 0:1, :], (lists, 128)) == window
    rank = jnp.dot(
        jnp.where(hit, 1.0, 0.0).astype(BF16),
        jnp.where(upper, 1.0, 0.0).astype(BF16),
        preferred_element_type=F32,
    ).astype(jnp.int32)
    side = jnp.where(rank >= half_cap, 1, 0)
    place = ((side * lists + window) * half_cap + (rank - side * half_cap)) * per
    place = jnp.sum(jnp.where(hit, place.astype(F32), 0.0), axis=0, keepdims=True)
    places_ref[...] = jnp.broadcast_to(place.astype(jnp.int32), places_ref.shape)


def slot_table(desc, acts, halo, half_cap, per):
    S = desc.shape[0] * half_cap
    acts, halo = (pltpu.with_memory_space_constraint(a, pltpu.VMEM) for a in (acts, halo))
    vm = pl.BlockSpec(memory_space=pltpu.VMEM)
    return pl.pallas_call(
        functools.partial(slot_kernel, half_cap, per),
        out_shape=(
            jax.ShapeDtypeStruct((S, 128), jnp.int32),
            jax.ShapeDtypeStruct((8, 128), jnp.int32),
            jax.ShapeDtypeStruct((25 * S, acts.shape[1]), BF16),
        ),
        in_specs=[vm, vm, vm],
        out_specs=(vm, vm, vm),
        scratch_shapes=[pltpu.VMEM((3, S, 128), jnp.int32)],
        compiler_params=pltpu.CompilerParams(vmem_limit_bytes=4 * 1024 * 1024),
        cost_estimate=pl.CostEstimate(
            flops=50 * S * acts.shape[1] * (acts.shape[0] + REACH), bytes_accessed=2_000_000, transcendentals=0
        ),
        name="slot_table",
    )(desc, acts, halo)


def trunk_kernel(
    slots,
    width,
    genome,
    slots_ref,
    early_ref,
    pair_ref,
    delta_ref,
    gain1_ref,
    gain2_ref,
    bias_ref,
    pair_bias_ref,
    conv1_ref,
    proj1_ref,
    conv2_ref,
    proj2_ref,
    head_ref,
    pair_head_ref,
    out_ref,
    xg,
    xalt,
    n1,
    g,
    h1,
    n2,
    h2,
    packed,
):
    S = slots
    C = early_ref.shape[1]
    half = proj1_ref.shape[0]
    tracks = head_ref.shape[1]
    here = lax.axis_index("seq")
    core = lax.rem(lax.axis_index("rep"), 2)
    other = 1 - core

    offset = slots_ref[:, 0:1]
    code = slots_ref[:, 1:2]
    where_bin = here * width + offset

    def inside(j, m):
        at = where_bin + (j * D1 + m * D2)
        return (at >= 0) & (at < genome)

    chosen = pick_rows(offset, pair_ref.shape[0], other * (REACH + width))
    for n in range(C // NT):
        at = pl.ds(n * NT, NT)
        found = jnp.dot(chosen, pair_ref[:, at], preferred_element_type=F32)
        xg[:, at] = (found + early_ref[:, at].astype(F32)).astype(BF16)
    bump = jnp.zeros((S, C), F32)
    for k in range(4):
        bump = jnp.where(code == k, delta_ref[k : k + 1, :].astype(F32), bump)
    xalt[...] = xg[12 * S : 13 * S, :].astype(F32) + bump

    def normed(values, gain):
        scale = lax.rsqrt(jnp.mean(values * values, axis=-1, keepdims=True) + EPS)
        return (values * scale * gain).astype(BF16)

    gain1 = gain1_ref[...].astype(F32).reshape(1, C)
    for b in range(25):
        n1[b * S : (b + 1) * S, :] = normed(xg[b * S : (b + 1) * S, :].astype(F32), gain1)
    n1[25 * S : 26 * S, :] = normed(xalt[...], gain1)

    for n in range(half // NT):
        at = pl.ds(n * NT, NT)
        taps = []
        for k in range(3):
            left = jnp.concatenate(
                [n1[k * 5 * S : (k + 3) * 5 * S, :], n1[25 * S : 26 * S, :]], axis=0
            )
            taps.append(jnp.dot(left, conv1_ref[k, :, at], preferred_element_type=F32))
        total = (taps[0] + taps[1]) + taps[2]
        g[: 15 * S, at] = gelu(total[: 15 * S]).astype(BF16)
        for j in range(3):
            base = (j * 5 + 2) * S
            parts = [
                taps[k][15 * S : 16 * S] if k == 2 - j else taps[k][base : base + S]
                for k in range(3)
            ]
            g[(15 + j) * S : (16 + j) * S, at] = gelu((parts[0] + parts[1]) + parts[2]).astype(BF16)

    for n in range(C // NT):
        at = pl.ds(n * NT, NT)
        delta = jnp.dot(g[...], proj1_ref[:, at], preferred_element_type=F32)
        for j in range(3):
            for m in range(5):
                b = j * 5 + m
                x = xg[(b + 5) * S : (b + 6) * S, at].astype(F32)
                h = jnp.where(inside(j - 1, m - 2), x + delta[b * S : (b + 1) * S], 0.0)
                h1[(m * 3 + j) * S : (m * 3 + j + 1) * S, at] = h.astype(BF16)
            b = 15 + j
            x = xalt[:, at] if j == 1 else xg[(j * 5 + 7) * S : (j * 5 + 8) * S, at].astype(F32)
            h = jnp.where(inside(j - 1, 0), x + delta[b * S : (b + 1) * S], 0.0)
            h1[b * S : (b + 1) * S, at] = h.astype(BF16)
    gain2 = gain2_ref[...].astype(F32).reshape(1, C)
    for b in range(18):
        n2[b * S : (b + 1) * S, :] = normed(h1[b * S : (b + 1) * S, :].astype(F32), gain2)

    for n in range(half // NT):
        at = pl.ds(n * NT, NT)
        taps = []
        for k in range(3):
            left = jnp.concatenate(
                [n2[k * 3 * S : (k + 3) * 3 * S, :], n2[15 * S : 18 * S, :]], axis=0
            )
            taps.append(jnp.dot(left, conv2_ref[k, :, at], preferred_element_type=F32))
        total = (taps[0] + taps[1]) + taps[2]
        g[: 9 * S, at] = gelu(total[: 9 * S]).astype(BF16)
        for i in range(3):
            base = i * 3 * S
            parts = [
                taps[k][9 * S : 12 * S] if k == 2 - i else taps[k][base : base + 3 * S]
                for k in range(3)
            ]
            g[(9 + 3 * i) * S : (12 + 3 * i) * S, at] = gelu(
                (parts[0] + parts[1]) + parts[2]
            ).astype(BF16)

    for n in range(C // NT):
        at = pl.ds(n * NT, NT)
        delta = jnp.dot(g[...], proj2_ref[:, at], preferred_element_type=F32)
        for i in range(3):
            plain = h1[(i + 1) * 3 * S : (i + 2) * 3 * S, at].astype(F32)
            changed = h1[15 * S : 18 * S, at].astype(F32) if i == 1 else plain
            lo = i * 3 * S
            h2[lo : lo + 3 * S, at] = (plain + delta[lo : lo + 3 * S]).astype(BF16)
            lo += 9 * S
            h2[lo : lo + 3 * S, at] = (changed + delta[lo : lo + 3 * S]).astype(BF16)

    keep = [
        jnp.where(inside(j - 1, i - 1), 1.0, 0.0) for i in range(3) for j in range(3)
    ]
    for side in range(2):
        bias = (bias_ref, pair_bias_ref)[side][...].astype(F32).reshape(1, tracks)
        weight = (head_ref, pair_head_ref)[side]
        block = (core if side == 0 else other) * (S * (tracks // 128))
        for n in range(tracks // NT):
            at = pl.ds(n * NT, NT)
            logits = jnp.dot(h2[...], weight[:, at], preferred_element_type=F32)
            cover = softplus(logits + bias[:, n * NT : (n + 1) * NT])
            score = jnp.zeros((S, NT), F32)
            for b in range(9):
                change = cover[(9 + b) * S : (10 + b) * S] - cover[b * S : (b + 1) * S]
                score = score + change * keep[b]
            per = tracks // 128
            for t in range(NT // 128):
                start = block + n * (NT // 128) + t
                packed[pl.ds(start, S, stride=per), :] = score[:, t * 128 : (t + 1) * 128]
    out_ref[...] = packed[...].astype(BF16)


def trunk_and_head(table, early, pair, delta, gain1, gain2, bias, pair_bias, weights, width, genome):
    conv1, proj1, conv2, proj2, head, pair_head = weights
    S = table.shape[0]
    C = early.shape[1]
    half = proj1.shape[0]
    tracks = head.shape[1]
    vm = pl.BlockSpec(memory_space=pltpu.VMEM)
    macs = S * (48 * C * half + 18 * C * half + 36 * C * half + 18 * C * half + 36 * C * tracks)
    operands = [
        pltpu.with_memory_space_constraint(a, pltpu.VMEM)
        for a in (table, early, pair, delta, gain1, gain2, bias, pair_bias) + weights
    ]
    return pl.pallas_call(
        functools.partial(trunk_kernel, S, width, genome),
        out_shape=jax.ShapeDtypeStruct((2 * S * tracks // 128, 128), BF16),
        in_specs=[vm] * len(operands),
        out_specs=vm,
        scratch_shapes=[
            pltpu.VMEM((25 * S, C), BF16),
            pltpu.VMEM((S, C), F32),
            pltpu.VMEM((26 * S, C), BF16),
            pltpu.VMEM((18 * S, half), BF16),
            pltpu.VMEM((18 * S, C), BF16),
            pltpu.VMEM((18 * S, C), BF16),
            pltpu.VMEM((18 * S, C), BF16),
            pltpu.VMEM((2 * S * tracks // 128, 128), F32),
        ],
        compiler_params=pltpu.CompilerParams(vmem_limit_bytes=12 * 1024 * 1024),
        cost_estimate=pl.CostEstimate(
            flops=2 * macs, bytes_accessed=28 * 1024 * 1024, transcendentals=S * 18 * (half * 2 + tracks * 4)
        ),
        name="trunk_and_head",
    )(*operands)


def return_kernel(places_ref, got_ref, out_ref, wide, tiles):
    wide[...] = got_ref[...].astype(F32)
    count, tracks = out_ref.shape
    per = tracks // 128
    for v in range(count):
        row = pl.multiple_of(places_ref[v], 8)
        tiles[v * per : (v + 1) * per, :] = wide[pl.ds(row, per), :]
    for t in range(per):
        out_ref[:, t * 128 : (t + 1) * 128] = tiles[pl.ds(t, count, stride=per), :]


def first_kernel(acts_ref, owners_ref, offsets_ref, codes_ref, edge_ref, out_ref, rows, sem):
    core = lax.rem(lax.axis_index("rep"), 2)
    count = owners_ref.shape[1]
    reach = edge_ref.shape[0]
    begin = pl.multiple_of((1 - core) * (acts_ref.shape[0] - reach), 16)
    copies = [pltpu.make_async_copy(acts_ref.at[pl.ds(begin, reach)], edge_ref, sem.at[3])]
    copies += [
        pltpu.make_async_copy(ref, row, sem.at[i])
        for i, (ref, row) in enumerate(zip((owners_ref, offsets_ref, codes_ref), rows))
    ]
    for copy in copies:
        copy.start()
    out_ref[...] = jnp.full(out_ref.shape, -1, jnp.int32)
    for copy in copies[1:]:
        copy.wait()
    for f in range(3):
        out_ref[f : f + 1, 0:count] = rows[f][...].reshape(1, count)
    copies[0].wait()


def edge_and_list(acts, owner, offsets, codes):
    hbm = pl.BlockSpec(memory_space=pltpu.HBM)
    vm = pl.BlockSpec(memory_space=pltpu.VMEM)
    args = [pltpu.with_memory_space_constraint(a, pltpu.HBM) for a in (acts, owner, offsets, codes)]
    return pl.pallas_call(
        first_kernel,
        out_shape=(
            jax.ShapeDtypeStruct((REACH, acts.shape[1]), BF16),
            jax.ShapeDtypeStruct((8, 128), jnp.int32),
        ),
        in_specs=[hbm, hbm, hbm, hbm],
        out_specs=(vm, vm),
        scratch_shapes=[
            [pltpu.VMEM(a.shape, jnp.int32) for a in args[1:]],
            pltpu.SemaphoreType.DMA((4,)),
        ],
        compiler_params=pltpu.CompilerParams(vmem_limit_bytes=2 * 1024 * 1024),
        cost_estimate=pl.CostEstimate(flops=1_000, bytes_accessed=900_000, transcendentals=0),
        name="edge_and_list",
    )(*args)


def spread_kernel(list_ref, out_ref):
    for s in range(out_ref.shape[0]):
        out_ref[s] = list_ref[...]


def spread(fields, lists):
    vm = pl.BlockSpec(memory_space=pltpu.VMEM)
    return pl.pallas_call(
        spread_kernel,
        out_shape=jax.ShapeDtypeStruct((lists, 8, 128), jnp.int32),
        in_specs=[vm],
        out_specs=vm,
        compiler_params=pltpu.CompilerParams(vmem_limit_bytes=1024 * 1024),
        cost_estimate=pl.CostEstimate(flops=20_000_000_000, bytes_accessed=40_000, transcendentals=0),
        name="spread_list",
    )(pltpu.with_memory_space_constraint(fields, pltpu.VMEM))


def per_device(
    reference_acts,
    owners,
    offsets,
    codes,
    base_delta,
    gain_one,
    conv_one,
    proj_one,
    gain_two,
    conv_two,
    proj_two,
    head_weight,
    head_bias,
):
    n_seq = lax.axis_size("seq")
    n_rep = lax.axis_size("rep")
    width = reference_acts.shape[0]
    genome = width * n_seq
    vcount = owners.shape[0]
    half_cap = max(2, 2 * vcount // n_seq) // 2
    tracks = head_weight.shape[1]
    swap = [(r, r ^ 1) for r in range(n_rep)]
    steps = [(i, r, i + 1 - 2 * (r % 2)) for i in range(n_seq) for r in range(n_rep)]
    edges = [(i * n_rep + r, j * n_rep + r) for i, r, j in steps if 0 <= j < n_seq]

    edge, fields = edge_and_list(reference_acts, owners.reshape(1, vcount), offsets, codes)
    fields = spread(fields, n_seq)
    halo = lax.ppermute(edge, ("seq", "rep"), edges)
    late_head, edge = lax.optimization_barrier((head_weight, edge))
    pair_head = lax.ppermute(late_head, "rep", swap)
    pair_bias = lax.ppermute(head_bias, "rep", swap)
    desc = lax.all_to_all(fields, "seq", split_axis=0, concat_axis=0, tiled=True)
    halo, desc = lax.optimization_barrier((halo, desc))
    pair = lax.ppermute(halo, "rep", swap)
    per = tracks // 128
    slots, places, early = slot_table(desc, reference_acts, halo, half_cap, per)
    scores = trunk_and_head(
        slots,
        early,
        pair,
        base_delta,
        gain_one,
        gain_two,
        head_bias,
        pair_bias,
        (conv_one, proj_one, conv_two, proj_two, head_weight, pair_head),
        width,
        genome,
    )
    groups = [
        [s * n_rep + x + c for c in range(2) for s in range(n_seq)] for x in range(0, n_rep, 2)
    ]
    got = lax.all_to_all(
        scores.reshape(2 * n_seq, half_cap * per, 128),
        ("seq", "rep"),
        split_axis=0,
        concat_axis=0,
        axis_index_groups=groups,
        tiled=True,
    ).reshape(2 * n_seq * half_cap * per, 128)
    got = pltpu.with_memory_space_constraint(got, pltpu.VMEM)
    return pl.pallas_call(
        return_kernel,
        out_shape=jax.ShapeDtypeStruct((vcount, tracks), F32),
        in_specs=[pl.BlockSpec(memory_space=pltpu.SMEM), pl.BlockSpec(memory_space=pltpu.VMEM)],
        out_specs=pl.BlockSpec(memory_space=pltpu.VMEM),
        scratch_shapes=[pltpu.VMEM(got.shape, F32), pltpu.VMEM((vcount * per, 128), F32)],
        compiler_params=pltpu.CompilerParams(vmem_limit_bytes=2 * 1024 * 1024),
        name="pick_scores",
    )(places[0], got)


def solution(mesh):
    return jax.shard_map(
        per_device,
        mesh=mesh,
        in_specs=(
            P("seq", None),
            P("seq", None),
            P("seq"),
            P("seq"),
            P(),
            P(),
            P(),
            P(),
            P(),
            P(),
            P(),
            P(None, "rep"),
            P("rep"),
        ),
        out_specs=P("seq", "rep"),
        check_vma=False,
    )
```
